32 devices in a mesh: ctx: 8 (over y, x, core), wt: 4 (over z).
Axes of the slice: x: 2, y: 2, z: 4, core: 2. Of those that a mesh axis runs over, the one named last changes fastest.
Arguments:
- block_in: float32 [4, 1024, 896], P('wt', 'ctx'), may hold values from -6 to 6
- cotangent: float32 [4, 1024, 896], P('wt', 'ctx'), may hold values from -12 to 12
- pairs: int32 [8], replicated, may hold values from 0 to 7, as said below
- positions: int32 [4, 1024], P('wt', 'ctx'), may hold values from 0 to 1023, as said below
- params: float32 [4, 3728096], P('wt'), may hold values from -16 to 16
- moment1: float32 [4, 3728096], P('wt', 'ctx'), may hold values from -100000 to 100000
- moment2: float32 [4, 3728096], P('wt', 'ctx'), may hold values from 0 to 10000000000, as said below
Outputs:
- block_out: float32 [4, 1024, 896], P('wt', 'ctx')
- input_grad: float32 [4, 1024, 896], P('wt', 'ctx')
- param_grad: float32 [4, 3728096], P('wt', 'ctx')
- new_params: float32 [4, 3728096], P('wt', 'ctx')
- new_moment1: float32 [4, 3728096], P('wt', 'ctx')
- new_moment2: float32 [4, 3728096], P('wt', 'ctx')
The draws below stay inside these ranges and needn't reach their ends.
Inputs may be any that keep to these rules, and one draw needn't show every extreme that they name: a permutation of 0 to 7; context index c holds blocks pairs[c] and 15 - pairs[c] of 64 tokens of every sequence. positions equals order, the causal position that pairs gives each row. `moment2`: positive.
All inputs are finite; a program needn't handle non-finite values.
Results may differ from the reference program's by a relative error of at most 0.012.
The reference program's roundings to bfloat16 on the way count: a program that leaves them out, or rounds other values in their place, can miss the bound.
Values may be sent and summed in bfloat16 or wider, within the bound.
A program may use at most 256 MiB of HBM per device.

```python
import math
import jax
import jax.numpy as jnp
from jax import lax

D = 896
QUERY_HEADS = 14
KEY_VALUE_HEADS = 2
HEAD_SIZE = 64
FF = 4864
TOK_DEV = 128
QW = 896
KEY_FEATURES = 128
HALF = 64
SEQUENCE_TOKENS = 1024
SHARD = 3728096
N_CTX = 8
N_WT = 4


def mirror_pairs(key):
    return jax.random.permutation(jax.random.fold_in(key, 11), N_CTX).astype(jnp.int32)


def draw_pairs(key, part):
    return mirror_pairs(key)


def draw_positions(key, part):
    chosen_pairs = mirror_pairs(key)
    row_ids = jnp.arange(SEQUENCE_TOKENS, dtype=jnp.int32)
    ctx_ids = row_ids // TOK_DEV
    local_row = row_ids % TOK_DEV
    chosen = jnp.sum(jnp.where(ctx_ids[:, None] == jnp.arange(N_CTX, dtype=jnp.int32)[None, :], chosen_pairs[None, :], 0), 1)
    block_id = jnp.where(local_row < HALF, chosen, 2 * N_CTX - 1 - chosen)
    order = (block_id * HALF + local_row % HALF).astype(jnp.int32)
    return jnp.broadcast_to(order[None, :], (N_WT, SEQUENCE_TOKENS)).astype(jnp.int32)


def draw_cotangent(key, part):
    noise = jax.random.truncated_normal(jax.random.fold_in(key, 51), -4.0, 4.0, (N_WT, SEQUENCE_TOKENS, D), jnp.float32)
    ratio_log = math.log(3.0)
    spread_pos = jnp.arange(N_WT, dtype=jnp.float32) / max(N_WT - 1, 1) - 0.5
    seq_scale = jnp.exp(ratio_log * spread_pos)
    return noise * seq_scale[:, None, None]


def shard_bounds_drawn():
    shapes = [(D, 0), (D, QW), (QW, 0), (D, KEY_FEATURES), (KEY_FEATURES, 0), (D, KEY_FEATURES), (KEY_FEATURES, 0), (QW, D), (D, 0), (FF, D), (FF, D), (FF, D)]
    bounds = [0]
    for rows_full, cols in shapes:
        length = rows_full // N_WT
        if cols > 0:
            length = length * cols
        bounds.append(bounds[-1] + length)
    return bounds


def layout_ids():
    bounds = shard_bounds_drawn()
    column = jnp.arange(SHARD, dtype=jnp.int32)
    segment = jnp.zeros((SHARD,), jnp.int32)
    for bound in bounds[1:12]:
        segment = segment + (column >= bound).astype(jnp.int32)
    return jnp.broadcast_to(segment[None, :], (N_WT, SHARD))


def pick_scale(segment, table):
    result = jnp.zeros(segment.shape, jnp.float32)
    for number in range(12):
        result = result + jnp.where(segment == number, table[number], 0.0)
    return result


def grad_scales():
    factor = math.sqrt(N_WT * SEQUENCE_TOKENS / 16384.0)
    return [15.0 * factor, 12.0 * factor, 12.0 * factor, 12.0 * factor, 12.0 * factor, 16.0 * factor, 800.0 * factor, 8.0 * factor, 40.0 * factor, 25.0 * factor, 20.0 * factor, 50.0 * factor]


def draw_params(key, part):
    segment = layout_ids()
    noise = jax.random.truncated_normal(jax.random.fold_in(key, 21), -4.0, 4.0, (N_WT, SHARD), jnp.float32)
    spreads = [0.1, 1.0 / math.sqrt(D), 0.08, 1.0 / math.sqrt(D), 0.08, 1.0 / math.sqrt(D), 0.05, 1.0 / math.sqrt(2 * HEAD_SIZE), 0.1, 1.0 / math.sqrt(D), 1.0 / math.sqrt(D), 1.0 / math.sqrt(FF)]
    values = noise * pick_scale(segment, spreads)
    is_gain = (segment == 0) | (segment == 8)
    return jnp.where(is_gain, 1.0 + values, values)


def draw_moment1(key, part):
    segment = layout_ids()
    noise = jax.random.truncated_normal(jax.random.fold_in(key, 31), -4.0, 4.0, (N_WT, SHARD), jnp.float32)
    return noise * 0.1 * pick_scale(segment, grad_scales())


def draw_moment2(key, part):
    segment = layout_ids()
    level = jax.random.uniform(jax.random.fold_in(key, 41), (N_WT, SHARD), jnp.float32, math.log(0.05), math.log(0.2))
    base = pick_scale(segment, grad_scales())
    return jnp.exp(level) * base * base


def levels(rng, extent, shards, low, top_value):
    def one(axis_at, blocks):
        steps = jax.random.uniform(jax.random.fold_in(jax.random.fold_in(rng, 6), axis_at), (blocks,), jnp.float32, low / len(shards), top_value / len(shards))
        return jnp.repeat(jnp.exp(steps), extent[axis_at] // blocks).reshape((-1,) + (1,) * (len(extent) - axis_at - 1))

    level = one(*shards[0])
    for cut in shards[1:]:
        level = level * one(*cut)
    return level


def centred(stream_key, extent, width, most, cuts=(), kind=jnp.bfloat16):
    level = levels(stream_key, extent, cuts, -0.22, 0.18) if cuts else 1.0
    entries = jax.random.normal(stream_key, extent, jnp.float32) * width * level
    return jnp.minimum(jnp.maximum(entries, -most), most).astype(kind)


def setup_inputs(seed: int = 0) -> dict:
    streams_of = jax.random.split(jax.random.key(seed), 8)
    block_in = centred(streams_of[0], (N_WT, SEQUENCE_TOKENS, D), 1.0, 6.0, ((0, 4), (1, 8)), jnp.float32)
    cotangent = draw_cotangent(jax.random.fold_in(streams_of[7], 71), 0)
    pairs = draw_pairs(jax.random.fold_in(streams_of[7], 71), 0)
    positions = draw_positions(jax.random.fold_in(streams_of[7], 71), 0)
    params = draw_params(jax.random.fold_in(streams_of[7], 71), 0)
    moment1 = draw_moment1(jax.random.fold_in(streams_of[7], 71), 0)
    moment2 = draw_moment2(jax.random.fold_in(streams_of[7], 71), 0)
    return dict(block_in=block_in, cotangent=cotangent, pairs=pairs, positions=positions, params=params, moment1=moment1, moment2=moment2)


theta_base = 1000000.0
norm_eps = 1e-06
beta_one = 0.9
beta_two = 0.95
adam_eps = 1e-08
learn_rate = 0.02
decay_rate = 0.1
step_count = 10.0

def piece_shapes():
    return [(D, 0), (D, QW), (QW, 0), (D, KEY_FEATURES), (KEY_FEATURES, 0), (D, KEY_FEATURES), (KEY_FEATURES, 0), (QW, D), (D, 0), (FF, D), (FF, D), (FF, D)]

def shard_bounds(parts):
    bounds = [0]
    for rows_full, cols in piece_shapes():
        length = rows_full // parts
        if cols > 0:
            length = length * cols
        bounds.append(bounds[-1] + length)
    return bounds

def unpack(rows_arr, parts, first, last):
    bounds = shard_bounds(parts)
    shapes = piece_shapes()
    count = rows_arr.shape[0]
    base = bounds[first]
    result = []
    for number in range(first, last):
        rows_full, cols = shapes[number]
        piece = rows_arr[:, bounds[number] - base:bounds[number + 1] - base]
        if cols > 0:
            result.append(piece.reshape(count * (rows_full // parts), cols))
        else:
            result.append(piece.reshape(-1))
    return result

def pack(pieces, parts):
    return jnp.concatenate([piece.reshape(parts, -1) for piece in pieces], 1)

def decay_mask(index_vec, parts):
    bounds = shard_bounds(parts)
    result = jnp.zeros(index_vec.shape, jnp.float32)
    for number in (1, 3, 5, 7, 9, 10, 11):
        inside = (index_vec >= bounds[number]) & (index_vec < bounds[number + 1])
        result = result + jnp.where(inside, 1.0, 0.0).astype(jnp.float32)
    return result

def rope_tables(position):
    freq_index = jnp.arange(HEAD_SIZE // 2, dtype=jnp.float32)
    inverse = jnp.exp(freq_index * (-2.0 * math.log(theta_base) / HEAD_SIZE))
    angles = position.astype(jnp.float32)[:, None] * inverse[None, :]
    cosine_table = jnp.cos(angles)
    sine_lookup = jnp.sin(angles)
    return (jnp.concatenate([cosine_table, cosine_table], 1), jnp.concatenate([sine_lookup, sine_lookup], 1))

def rotary_apply(values, cosine_table, sine_lookup):
    top_half = values[..., HEAD_SIZE // 2:]
    low_half = values[..., :HEAD_SIZE // 2]
    turned = jnp.concatenate([-top_half, low_half], -1)
    return values * cosine_table[:, None, :] + turned * sine_lookup[:, None, :]

def rotary_inverse(gradient, cosine_table, sine_lookup):
    scaled = gradient * sine_lookup[:, None, :]
    turned = jnp.concatenate([scaled[..., HEAD_SIZE // 2:], -scaled[..., :HEAD_SIZE // 2]], -1)
    return gradient * cosine_table[:, None, :] + turned

def causal_order(pairs):
    row_ids = jnp.arange(SEQUENCE_TOKENS, dtype=jnp.int32)
    ctx_ids = row_ids // TOK_DEV
    local_row = row_ids % TOK_DEV
    chosen = lax.optimization_barrier(jnp.sum(jnp.where(ctx_ids[:, None] == jnp.arange(N_CTX, dtype=jnp.int32)[None, :], pairs[None, :], 0), 1))
    block_id = jnp.where(local_row < HALF, chosen, 2 * N_CTX - 1 - chosen)
    return (block_id * HALF + local_row % HALF).astype(jnp.int32)

def outer_dot(left, right):
    return lax.dot_general(left, right, (((0,), (0,)), ((), ())), preferred_element_type=jnp.float32)

def inner_dot(left, right):
    return lax.dot_general(left, right, (((1,), (1,)), ((), ())), preferred_element_type=jnp.float32)

def feed_forward(mid_rows, cot_rows, gain_two, wg_b, wu_b, wd_b):
    gain_full = gain_two.astype(jnp.float32)
    inv_rms = lax.rsqrt(lax.optimization_barrier(jnp.mean(mid_rows * mid_rows, -1, keepdims=True)) + norm_eps)
    normed = (mid_rows * inv_rms * gain_full).astype(jnp.bfloat16)
    gate_pre = inner_dot(normed, wg_b)
    up_pre = inner_dot(normed, wu_b)
    sigmoid_gate = jax.nn.sigmoid(gate_pre)
    silu_gate = gate_pre * sigmoid_gate
    hidden_bf = (silu_gate * up_pre).astype(jnp.bfloat16)
    out_rows = mid_rows + jnp.dot(hidden_bf, wd_b, preferred_element_type=jnp.float32)
    cot_bf = cot_rows.astype(jnp.bfloat16)
    grad_wd = outer_dot(hidden_bf, cot_bf)
    d_hidden = inner_dot(cot_bf, wd_b)
    d_gate = (d_hidden * up_pre * sigmoid_gate * (1.0 + gate_pre * (1.0 - sigmoid_gate))).astype(jnp.bfloat16)
    d_up = (d_hidden * silu_gate).astype(jnp.bfloat16)
    grad_wg = outer_dot(d_gate, normed)
    grad_wu = outer_dot(d_up, normed)
    d_norm = jnp.dot(d_gate, wg_b, preferred_element_type=jnp.float32) + jnp.dot(d_up, wu_b, preferred_element_type=jnp.float32)
    grad_gain = lax.optimization_barrier(jnp.sum(d_norm * mid_rows * inv_rms, 0))
    d_scaled = d_norm * gain_full
    d_mid = cot_rows + inv_rms * d_scaled - mid_rows * (inv_rms * inv_rms * inv_rms) * lax.optimization_barrier(jnp.mean(d_scaled * mid_rows, -1, keepdims=True))
    return (out_rows, d_mid, grad_gain, grad_wg, grad_wu, grad_wd)

def reference(block_in, cotangent, pairs, positions, params, moment1, moment2):
    group = QUERY_HEADS // KEY_VALUE_HEADS
    score_scale = 1.0 / math.sqrt(HEAD_SIZE)
    all_rows = N_WT * SEQUENCE_TOKENS
    gain_b, wq_b, bq_b, wk_b, bk_b, wv_b, bv_b, wo_b, gain_two, wg_b, wu_b, wd_b = unpack(params.astype(jnp.bfloat16), N_WT, 0, 12)
    order_pos = causal_order(pairs)
    inverse_order = jnp.zeros((SEQUENCE_TOKENS,), jnp.int32).at[order_pos].set(jnp.arange(SEQUENCE_TOKENS, dtype=jnp.int32))
    x_rows = block_in[:, inverse_order].reshape(all_rows, D)
    cot_rows = cotangent[:, inverse_order].reshape(all_rows, D)
    rope_pos = positions[:, inverse_order].reshape(all_rows)
    gain_full = gain_b.astype(jnp.float32)
    inv_rms = lax.rsqrt(lax.optimization_barrier(jnp.mean(x_rows * x_rows, -1, keepdims=True)) + norm_eps)
    normed = (x_rows * inv_rms * gain_full).astype(jnp.bfloat16)
    queries = jnp.dot(normed, wq_b, preferred_element_type=jnp.float32) + bq_b.astype(jnp.float32)
    key_projected = jnp.dot(normed, wk_b, preferred_element_type=jnp.float32) + bk_b.astype(jnp.float32)
    value_projected = jnp.dot(normed, wv_b, preferred_element_type=jnp.float32) + bv_b.astype(jnp.float32)
    cosine_table, sine_lookup = rope_tables(rope_pos)
    query_narrow = rotary_apply(queries.reshape(all_rows, QUERY_HEADS, HEAD_SIZE), cosine_table, sine_lookup).astype(jnp.bfloat16)
    key_narrow = rotary_apply(key_projected.reshape(all_rows, KEY_VALUE_HEADS, HEAD_SIZE), cosine_table, sine_lookup).astype(jnp.bfloat16)
    value_narrow = value_projected.astype(jnp.bfloat16).reshape(all_rows, KEY_VALUE_HEADS, HEAD_SIZE)
    query_block = min(512, SEQUENCE_TOKENS)
    block_count = SEQUENCE_TOKENS // query_block
    query_wide = query_narrow.astype(jnp.float32).reshape(N_WT, block_count, query_block, KEY_VALUE_HEADS, group, HEAD_SIZE)
    k_float = key_narrow.astype(jnp.float32).reshape(N_WT, SEQUENCE_TOKENS, KEY_VALUE_HEADS, HEAD_SIZE)
    v_float = value_narrow.astype(jnp.float32).reshape(N_WT, SEQUENCE_TOKENS, KEY_VALUE_HEADS, HEAD_SIZE)
    start_offsets = jnp.arange(block_count, dtype=jnp.int32) * query_block
    key_ids = jnp.arange(SEQUENCE_TOKENS, dtype=jnp.int32)

    def block_scores(q_part, k_seq, start_row):
        scores = score_scale * jnp.einsum('qkgd,tkd->kgqt', q_part, k_seq)
        query_ids = start_row + jnp.arange(query_block, dtype=jnp.int32)
        visible = key_ids[None, :] <= query_ids[:, None]
        return (jnp.where(visible, scores, -jnp.inf), visible)

    def forward_sequence(inputs):
        q_seq, k_seq, v_seq = inputs

        def forward_block(block_inputs):
            q_part, start_row = block_inputs
            scores, visible = block_scores(q_part, k_seq, start_row)
            peak = lax.optimization_barrier(jnp.max(scores, -1, keepdims=True))
            log_sum = peak + jnp.log(lax.optimization_barrier(jnp.sum(jnp.exp(scores - peak), -1, keepdims=True)))
            probs_bf = jnp.where(visible, jnp.exp(scores - log_sum), 0.0).astype(jnp.bfloat16)
            context_part = jnp.einsum('kgqt,tkd->qkgd', probs_bf.astype(jnp.float32), v_seq)
            return (context_part, log_sum)
        return lax.map(forward_block, (q_seq, start_offsets))
    full_context, full_log_sum = lax.map(forward_sequence, (query_wide, k_float, v_float))
    context_rows = full_context.reshape(all_rows, QW)
    context_bf = context_rows.astype(jnp.bfloat16)
    mid_rows = x_rows + jnp.dot(context_bf, wo_b, preferred_element_type=jnp.float32)
    ff_rows = math.gcd(all_rows, 4096)
    ff_count = all_rows // ff_rows

    def ff_step(carry, inputs):
        mid_part, cot_part = inputs
        out_part, dmid_part, g_part, wg_part, wu_part, wd_part = feed_forward(mid_part, cot_part, gain_two, wg_b, wu_b, wd_b)
        carry = (carry[0] + g_part, carry[1] + wg_part, carry[2] + wu_part, carry[3] + wd_part)
        return (carry, (out_part, dmid_part))
    ff_init = (jnp.zeros((D,), jnp.float32), jnp.zeros((FF, D), jnp.float32), jnp.zeros((FF, D), jnp.float32), jnp.zeros((FF, D), jnp.float32))
    ff_sums, (out_blocks, dmid_blocks) = lax.scan(ff_step, ff_init, (mid_rows.reshape(ff_count, ff_rows, D), cot_rows.reshape(ff_count, ff_rows, D)))
    grad_gain_two, grad_wg, grad_wu, grad_wd = ff_sums
    out_rows = out_blocks.reshape(all_rows, D)
    d_mid = dmid_blocks.reshape(all_rows, D)
    d_mid_bf = d_mid.astype(jnp.bfloat16)
    grad_wo = outer_dot(context_bf, d_mid_bf)
    context_gradient = inner_dot(d_mid_bf, wo_b)
    context_gradient_narrow = context_gradient.astype(jnp.bfloat16)
    delta_rows = lax.optimization_barrier(jnp.sum((context_gradient * context_rows).reshape(all_rows, KEY_VALUE_HEADS, group, HEAD_SIZE), -1))
    gradient_wide = context_gradient_narrow.astype(jnp.float32).reshape(N_WT, block_count, query_block, KEY_VALUE_HEADS, group, HEAD_SIZE)
    block_deltas = delta_rows.reshape(N_WT, block_count, query_block, KEY_VALUE_HEADS, group)

    def backward_sequence(inputs):
        q_seq, g_seq, lse_seq, delta_seq, k_seq, v_seq = inputs

        def backward_block(carry, block_inputs):
            key_acc, value_acc = carry
            q_part, d_part, lse_part, delta_part, start_row = block_inputs
            scores, visible = block_scores(q_part, k_seq, start_row)
            probs = jnp.where(visible, jnp.exp(scores - lse_part), 0.0)
            probs_bf = probs.astype(jnp.bfloat16).astype(jnp.float32)
            d_probs = jnp.einsum('qkgd,tkd->kgqt', d_part, v_seq)
            delta_t = jnp.transpose(delta_part, (1, 2, 0))[..., None]
            d_scores = (probs * (d_probs - delta_t)).astype(jnp.bfloat16).astype(jnp.float32)
            d_query = score_scale * jnp.einsum('kgqt,tkd->qkgd', d_scores, k_seq)
            key_acc = key_acc + score_scale * jnp.einsum('kgqt,qkgd->tkd', d_scores, q_part)
            value_acc = value_acc + jnp.einsum('kgqt,qkgd->tkd', probs_bf, d_part)
            return ((key_acc, value_acc), d_query)
        empty_rows = jnp.zeros((SEQUENCE_TOKENS, KEY_VALUE_HEADS, HEAD_SIZE), jnp.float32)
        (key_acc, value_acc), d_query = lax.scan(backward_block, (empty_rows, empty_rows), (q_seq, g_seq, lse_seq, delta_seq, start_offsets))
        return (d_query, key_acc, value_acc)
    query_blocks, rotated_keys, value_sums = lax.map(backward_sequence, (query_wide, gradient_wide, full_log_sum, block_deltas, k_float, v_float))
    d_query = rotary_inverse(query_blocks.reshape(all_rows, QUERY_HEADS, HEAD_SIZE), cosine_table, sine_lookup).reshape(all_rows, QW)
    key_gradient = rotary_inverse(rotated_keys.reshape(all_rows, KEY_VALUE_HEADS, HEAD_SIZE), cosine_table, sine_lookup).reshape(all_rows, KEY_FEATURES)
    value_gradient = value_sums.reshape(all_rows, KEY_FEATURES)
    dq_bf = d_query.astype(jnp.bfloat16)
    dk_bf = key_gradient.astype(jnp.bfloat16)
    dv_bf = value_gradient.astype(jnp.bfloat16)
    grad_wq = outer_dot(normed, dq_bf)
    grad_wk = outer_dot(normed, dk_bf)
    grad_wv = outer_dot(normed, dv_bf)
    d_norm = inner_dot(dq_bf, wq_b) + inner_dot(dk_bf, wk_b) + inner_dot(dv_bf, wv_b)
    grad_gain = lax.optimization_barrier(jnp.sum(d_norm * x_rows * inv_rms, 0))
    d_scaled = d_norm * gain_full
    d_input = inv_rms * d_scaled - x_rows * (inv_rms * inv_rms * inv_rms) * lax.optimization_barrier(jnp.mean(d_scaled * x_rows, -1, keepdims=True))
    grad_rows = d_mid + d_input
    param_grad = pack([grad_gain, grad_wq, lax.optimization_barrier(jnp.sum(dq_bf.astype(jnp.float32), 0)), grad_wk, lax.optimization_barrier(jnp.sum(dk_bf.astype(jnp.float32), 0)), grad_wv, lax.optimization_barrier(jnp.sum(dv_bf.astype(jnp.float32), 0)), grad_wo, grad_gain_two, grad_wg, grad_wu, grad_wd], N_WT)
    new_moment1 = beta_one * moment1 + (1.0 - beta_one) * param_grad
    new_moment2 = beta_two * moment2 + (1.0 - beta_two) * param_grad * param_grad
    m_hat = new_moment1 / (1.0 - beta_one ** step_count)
    v_hat = new_moment2 / (1.0 - beta_two ** step_count)
    decay = decay_mask(jnp.arange(SHARD, dtype=jnp.int32), N_WT)[None, :]
    new_params = params - learn_rate * (m_hat / (jnp.sqrt(v_hat) + adam_eps) + decay_rate * decay * params)
    block_out = out_rows.reshape(N_WT, SEQUENCE_TOKENS, D)[:, order_pos]
    input_grad = grad_rows.reshape(N_WT, SEQUENCE_TOKENS, D)[:, order_pos]
    return (block_out, input_grad, param_grad, new_params, new_moment1, new_moment2)
```

```python
import math

import jax
import jax.numpy as jnp
from jax import lax
from jax.experimental import pallas as pl
from jax.experimental.pallas import tpu as pltpu
from jax.sharding import PartitionSpec as P

D = 896
QUERY_HEADS = 14
KEY_VALUE_HEADS = 2
HEAD_SIZE = 64
FF = 4864
QW = 896
KEY_FEATURES = 128


theta_base = 1000000.0
norm_eps = 1e-06
beta_one = 0.9
beta_two = 0.95
adam_eps = 1e-08
learn_rate = 0.02
decay_rate = 0.1
step_count = 10.0


def piece_shapes():
    return [
        (D, 0),
        (D, QW),
        (QW, 0),
        (D, KEY_FEATURES),
        (KEY_FEATURES, 0),
        (D, KEY_FEATURES),
        (KEY_FEATURES, 0),
        (QW, D),
        (D, 0),
        (FF, D),
        (FF, D),
        (FF, D),
    ]


def shard_bounds(parts):
    bounds = [0]
    for rows_full, cols in piece_shapes():
        length = rows_full // parts
        if cols > 0:
            length = length * cols
        bounds.append(bounds[-1] + length)
    return bounds


def unpack(rows_arr, parts, first, last):
    bounds = shard_bounds(parts)
    shapes = piece_shapes()
    count = rows_arr.shape[0]
    base = bounds[first]
    result = []
    for number in range(first, last):
        rows_full, cols = shapes[number]
        piece = rows_arr[:, bounds[number] - base : bounds[number + 1] - base]
        if cols > 0:
            result.append(piece.reshape(count * (rows_full // parts), cols))
        else:
            result.append(piece.reshape(-1))
    return result


def decay_mask(index_vec, parts):
    bounds = shard_bounds(parts)
    result = jnp.zeros(index_vec.shape, jnp.float32)
    for number in (1, 3, 5, 7, 9, 10, 11):
        inside = (index_vec >= bounds[number]) & (index_vec < bounds[number + 1])
        result = result + jnp.where(inside, 1.0, 0.0).astype(jnp.float32)
    return result


def rope_tables(position):
    freq_index = jnp.arange(HEAD_SIZE // 2, dtype=jnp.float32)
    inverse = jnp.exp(freq_index * (-2.0 * math.log(theta_base) / HEAD_SIZE))
    angles = position.astype(jnp.float32)[:, None] * inverse[None, :]
    cosine_table = jnp.cos(angles)
    sine_lookup = jnp.sin(angles)
    return (
        jnp.concatenate([cosine_table, cosine_table], 1),
        jnp.concatenate([sine_lookup, sine_lookup], 1),
    )


def rotary_apply(values, cosine_table, sine_lookup):
    top_half = values[..., HEAD_SIZE // 2 :]
    low_half = values[..., : HEAD_SIZE // 2]
    turned = jnp.concatenate([-top_half, low_half], -1)
    return values * cosine_table[:, None, :] + turned * sine_lookup[:, None, :]


def rotary_inverse(gradient, cosine_table, sine_lookup):
    scaled = gradient * sine_lookup[:, None, :]
    turned = jnp.concatenate([scaled[..., HEAD_SIZE // 2 :], -scaled[..., : HEAD_SIZE // 2]], -1)
    return gradient * cosine_table[:, None, :] + turned


def lookup(table, index_vec):
    slots = jnp.arange(table.shape[0], dtype=jnp.int32)
    return jnp.sum(jnp.where(index_vec[..., None] == slots, table, 0), -1)


def outer_dot(left, right):
    return lax.dot_general(
        left, right, (((0,), (0,)), ((), ())), preferred_element_type=jnp.float32
    )


def inner_dot(left, right):
    return lax.dot_general(
        left, right, (((1,), (1,)), ((), ())), preferred_element_type=jnp.float32
    )


def gate_terms(gate_pre, up_pre, d_hidden):
    sigmoid_gate = jax.nn.sigmoid(gate_pre)
    silu_gate = gate_pre * sigmoid_gate
    d_gate = (d_hidden * up_pre * sigmoid_gate * (1.0 + gate_pre * (1.0 - sigmoid_gate))).astype(
        jnp.bfloat16
    )
    d_up = (d_hidden * silu_gate).astype(jnp.bfloat16)
    return (d_gate, d_up)


def hidden_units(gate_pre, up_pre):
    return (gate_pre * jax.nn.sigmoid(gate_pre) * up_pre).astype(jnp.bfloat16)


LANES = 128
COLUMN_TILES = D // LANES
VMEM_BYTES = 56 * 1024 * 1024
MATRIX_COLS = QW + 2 * KEY_FEATURES + D


def big_pieces(parts):
    bounds = shard_bounds(parts)
    row_count = D // parts
    return [
        (bounds[1], row_count, COLUMN_TILES, 0),
        (bounds[3], row_count, 1, QW),
        (bounds[5], row_count, 1, QW + KEY_FEATURES),
        (bounds[7], row_count, COLUMN_TILES, QW + 2 * KEY_FEATURES),
    ]


def chunk_rows(rows):
    return 32 if rows % 32 == 0 else 16


def lane_ids(rows):
    return lax.broadcasted_iota(jnp.int32, (rows, LANES), 1)


def unpack_kernel(parts, flat_ref, attn_ref, wg_ref, wu_ref, wd_ref, held):
    bounds = shard_bounds(parts)

    def extract(base, rows, tiles, out_ref, column):
        step = chunk_rows(rows)
        flat_rows = step * tiles
        first, lane = base // LANES, base % LANES

        def chunk(number, carry):
            at = first + number * flat_rows
            if lane:
                low = pltpu.roll(flat_ref[pl.ds(at, flat_rows), :], LANES - lane, 1)
                high = pltpu.roll(flat_ref[pl.ds(at + 1, flat_rows), :], LANES - lane, 1)
                block = jnp.where(lane_ids(flat_rows) < LANES - lane, low, high)
            else:
                block = flat_ref[pl.ds(at, flat_rows), :]
            out_rows = pl.ds(pl.multiple_of(number * step, step), step)
            if tiles == 1:
                out_ref[out_rows, column : column + LANES] = block.astype(jnp.bfloat16)
            else:
                held[0:flat_rows, :] = block
                for tile in range(tiles):
                    part = held[pl.ds(tile, step, stride=tiles), :]
                    left = column + tile * LANES
                    out_ref[out_rows, left : left + LANES] = part.astype(jnp.bfloat16)
            return carry

        lax.fori_loop(0, rows // step, chunk, 0)

    for base, rows, tiles, column in big_pieces(parts):
        extract(base, rows, tiles, attn_ref, column)
    for number, out_ref in ((9, wg_ref), (10, wu_ref), (11, wd_ref)):
        extract(bounds[number], FF // parts, COLUMN_TILES, out_ref, 0)


def unpack_weights(flat_rows, parts):
    whole = pl.BlockSpec(memory_space=pltpu.VMEM)
    ff_rows = FF // parts
    return pl.pallas_call(
        lambda *refs: unpack_kernel(parts, *refs),
        out_shape=(
            jax.ShapeDtypeStruct((D // parts, MATRIX_COLS), jnp.bfloat16),
            jax.ShapeDtypeStruct((ff_rows, D), jnp.bfloat16),
            jax.ShapeDtypeStruct((ff_rows, D), jnp.bfloat16),
            jax.ShapeDtypeStruct((ff_rows, D), jnp.bfloat16),
        ),
        in_specs=[whole],
        out_specs=(whole,) * 4,
        scratch_shapes=[pltpu.VMEM((32 * COLUMN_TILES, LANES), jnp.float32)],
        compiler_params=pltpu.CompilerParams(vmem_limit_bytes=VMEM_BYTES),
    )(flat_rows)


def small_rows(vectors, bases):
    rows = []
    where_rows = []
    for vector, base in zip(vectors, bases):
        lane = base % LANES
        end = lane + vector.shape[0]
        padded = jnp.pad(vector, (lane, -end % LANES)).reshape(-1, LANES)
        for extra in range(padded.shape[0]):
            where_rows.append(base // LANES + extra)
        rows.append(padded)
    stacked = jnp.concatenate(rows, 0)
    return jnp.pad(stacked, ((0, -stacked.shape[0] % 8), (0, 0))), where_rows


def ff_first_row(ctx_id, piece_len, prefix, total_rows, taken):
    rows = [
        min(max(0, (number * piece_len - prefix) // D // 16 * 16), total_rows - taken)
        for number in range(ctx_id)
    ]
    return rows


def assemble_kernel(
    parts, row_of_small, place_ref, small_ref, attn_ref, terms_ref, own_ref, grad_ref, param_ref,
    flat, held,
):
    senders, taken = terms_ref.shape[0], terms_ref.shape[1]
    prefix = shard_bounds(parts)[9]
    out_rows = grad_ref.shape[0]
    prefix_rows = prefix // LANES + 2
    flat[0:prefix_rows, :] = jnp.zeros((prefix_rows, LANES), jnp.float32)
    for number, row in enumerate(row_of_small):
        flat[row : row + 1, :] = flat[row : row + 1, :] + small_ref[number : number + 1, :]

    def insert(base, rows, tiles, load):
        step = 16
        flat_rows = step * tiles
        first, lane = base // LANES, base % LANES

        def chunk(number, carry):
            at = first + number * flat_rows
            for tile in range(tiles):
                part = load(pl.multiple_of(number * step, step), step, tile)
                if tiles == 1:
                    held[0:step, :] = part
                else:
                    held[pl.ds(tile, step, stride=tiles), :] = part
            block = held[0:flat_rows, :]
            if lane:
                block = pltpu.roll(block, lane, 1)
                ids = lane_ids(flat_rows)
                old = flat[pl.ds(at, flat_rows), :]
                flat[pl.ds(at, flat_rows), :] = jnp.where(ids < lane, old, block)
                old = flat[pl.ds(at + 1, flat_rows), :]
                flat[pl.ds(at + 1, flat_rows), :] = jnp.where(ids < lane, block, old)
            else:
                flat[pl.ds(at, flat_rows), :] = block
            return carry

        lax.fori_loop(0, rows // step, chunk, 0)

    def from_attn(column):
        def load(row, count, tile):
            left = column + tile * LANES
            return attn_ref[pl.ds(row, count), left : left + LANES]

        return load

    def from_terms(row, count, tile):
        columns = slice(tile * LANES, tile * LANES + LANES)
        total = terms_ref[0, pl.ds(row, count), columns].astype(jnp.float32)
        for sender in range(1, senders):
            total = total + terms_ref[sender, pl.ds(row, count), columns].astype(jnp.float32)
        return total

    for base, rows, tiles, column in big_pieces(parts):
        insert(base, rows, tiles, from_attn(column))
    insert(prefix, taken, COLUMN_TILES, from_terms)

    def shift(source, row_start, lane, out_ref):
        step = 64
        turn = (LANES - lane) % LANES

        def chunk(number, carry):
            at = row_start + number * step
            low = pltpu.roll(source[pl.ds(at, step), :], turn, 1)
            high = pltpu.roll(source[pl.ds(at + 1, step), :], turn, 1)
            out_ref[pl.ds(pl.multiple_of(number * step, step), step), :] = jnp.where(
                lane_ids(step) < LANES - lane, low, high
            )
            return carry

        lax.fori_loop(0, out_rows // step, chunk, 0)

    shift(flat, place_ref[0], place_ref[1], grad_ref)
    shift(own_ref, place_ref[2], place_ref[3], param_ref)


def assemble(parts, small, row_of_small, attn_sum, terms, own_rows, place, out_rows):
    whole = pl.BlockSpec(memory_space=pltpu.VMEM)
    prefix = shard_bounds(parts)[9]
    flat_rows = prefix // LANES + terms.shape[1] * COLUMN_TILES + out_rows // 8 * 8 + 80
    shape = jax.ShapeDtypeStruct((out_rows, LANES), jnp.float32)
    return pl.pallas_call(
        lambda *refs: assemble_kernel(parts, row_of_small, *refs),
        out_shape=(shape, shape),
        in_specs=[pl.BlockSpec(memory_space=pltpu.SMEM)] + [whole] * 4,
        out_specs=(whole, whole),
        scratch_shapes=[
            pltpu.VMEM((flat_rows, LANES), jnp.float32),
            pltpu.VMEM((16 * COLUMN_TILES, LANES), jnp.float32),
        ],
        compiler_params=pltpu.CompilerParams(vmem_limit_bytes=VMEM_BYTES),
    )(place, small, attn_sum, terms, own_rows)


def body(block_in, cotangent, pairs, positions, params, moment1, moment2):
    n_ctx = lax.axis_size("ctx")
    n_wt = lax.axis_size("wt")
    token_rows = block_in.shape[1]
    half_rows = token_rows // 2
    seq_len = token_rows * n_ctx
    key_tile = min(512, seq_len)
    query_group_width = QUERY_HEADS // KEY_VALUE_HEADS
    score_scale = 1.0 / math.sqrt(HEAD_SIZE)
    ctx_id = lax.axis_index("ctx")
    wt_id = lax.axis_index("wt")
    x_rows = block_in[0]
    cot_rows = cotangent[0]
    bounds = shard_bounds(n_wt)
    prefix = bounds[9]
    shard_len = params.shape[1]
    flat_params = jnp.pad(params[0], (0, -shard_len % 1024 + 10240)).reshape(-1, LANES)
    attn_own, wg_own, wu_own, wd_own = unpack_weights(flat_params, n_wt)
    vector_numbers = (0, 2, 4, 6, 8)
    vectors_own = jnp.concatenate(
        [params[0, bounds[number] : bounds[number + 1]] for number in vector_numbers]
    ).astype(jnp.bfloat16)
    attn_all = lax.all_gather(attn_own, "wt", axis=0, tiled=True)
    vectors_all = lax.all_gather(vectors_own, "wt", axis=0)
    wq_b = attn_all[:, :QW]
    wk_b = attn_all[:, QW : QW + KEY_FEATURES]
    wv_b = attn_all[:, QW + KEY_FEATURES : QW + 2 * KEY_FEATURES]
    wo_b = attn_all[:, QW + 2 * KEY_FEATURES :]
    vector_parts = []
    left = 0
    for number in vector_numbers:
        width = bounds[number + 1] - bounds[number]
        vector_parts.append(vectors_all[:, left : left + width].reshape(-1))
        left += width
    gain_b, bq_b, bk_b, bv_b, gain_two = vector_parts
    gain_full = gain_b.astype(jnp.float32)
    inv_rms = lax.rsqrt(jnp.mean(x_rows * x_rows, -1, keepdims=True) + norm_eps)
    normed = (x_rows * inv_rms * gain_full).astype(jnp.bfloat16)
    queries = jnp.dot(normed, wq_b, preferred_element_type=jnp.float32) + bq_b.astype(jnp.float32)
    key_projected = jnp.dot(normed, wk_b, preferred_element_type=jnp.float32) + bk_b.astype(
        jnp.float32
    )
    value_projected = jnp.dot(normed, wv_b, preferred_element_type=jnp.float32) + bv_b.astype(
        jnp.float32
    )
    cosine_table, sine_lookup = rope_tables(positions[0])
    query_narrow = rotary_apply(
        queries.reshape(token_rows, QUERY_HEADS, HEAD_SIZE), cosine_table, sine_lookup
    ).astype(jnp.bfloat16)
    key_narrow = rotary_apply(
        key_projected.reshape(token_rows, KEY_VALUE_HEADS, HEAD_SIZE), cosine_table, sine_lookup
    ).astype(jnp.bfloat16)
    value_narrow = value_projected.astype(jnp.bfloat16)
    own_kv = jnp.concatenate([key_narrow.reshape(token_rows, KEY_FEATURES), value_narrow], 1)
    all_kv = lax.all_gather(own_kv, "ctx", axis=0, tiled=True)
    block_ids = jnp.arange(2 * n_ctx, dtype=jnp.int32)
    target = jnp.where(block_ids < n_ctx, block_ids, 2 * n_ctx - 1 - block_ids)
    owner = jnp.sum(
        jnp.where(
            pairs[None, :] == target[:, None], jnp.arange(n_ctx, dtype=jnp.int32)[None, :], 0
        ),
        1,
    )
    late_side = (block_ids >= n_ctx).astype(jnp.int32)
    causal_ids = jnp.arange(seq_len, dtype=jnp.int32)
    block_of = causal_ids // half_rows
    source_row = (
        lookup(owner, block_of) * token_rows
        + lookup(late_side, block_of) * half_rows
        + causal_ids % half_rows
    )
    sorted_kv = jnp.take(all_kv, source_row, axis=0)
    early_block = lookup(pairs, ctx_id)
    late_block = 2 * n_ctx - 1 - early_block

    def query_positions(block_now):
        return block_now * half_rows + jnp.arange(half_rows, dtype=jnp.int32)

    def tile_total(block_now):
        return ((block_now + 1) * half_rows + key_tile - 1) // key_tile

    def key_slice(tile_no):
        tile_start = tile_no * key_tile
        key_value_tile = lax.dynamic_slice_in_dim(sorted_kv, tile_start, key_tile, 0)
        key_block_tile = key_value_tile[:, :KEY_FEATURES].reshape(
            key_tile, KEY_VALUE_HEADS, HEAD_SIZE
        )
        value_tile = key_value_tile[:, KEY_FEATURES:].reshape(key_tile, KEY_VALUE_HEADS, HEAD_SIZE)
        k_pos = tile_start + jnp.arange(key_tile, dtype=jnp.int32)
        return (tile_start, key_block_tile, value_tile, k_pos)

    def attend(query_half, block_now):
        q_pos = query_positions(block_now)
        query_group = query_half.reshape(half_rows, KEY_VALUE_HEADS, query_group_width, HEAD_SIZE)

        def tile_scores(tile_no):
            tile_start, key_block_tile, value_tile, k_pos = key_slice(tile_no)
            scores = score_scale * jnp.einsum(
                "qkgd,tkd->kgqt", query_group, key_block_tile, preferred_element_type=jnp.float32
            )
            visible = k_pos[None, :] <= q_pos[:, None]
            return (jnp.where(visible, scores, -jnp.inf), value_tile)

        def total_step(tile_no, state_carry):
            run_peak, run_total = state_carry
            scores, value_tile = tile_scores(tile_no)
            new_peak = jnp.maximum(run_peak, jnp.max(scores, -1))
            factor = jnp.exp(run_peak - new_peak)
            run_total = run_total * factor + jnp.sum(jnp.exp(scores - new_peak[..., None]), -1)
            return (new_peak, run_total)

        tile_count = tile_total(block_now)
        initial_state = (
            jnp.full((KEY_VALUE_HEADS, query_group_width, half_rows), -jnp.inf, jnp.float32),
            jnp.zeros((KEY_VALUE_HEADS, query_group_width, half_rows), jnp.float32),
        )
        run_peak, run_total = lax.fori_loop(0, tile_count, total_step, initial_state)
        log_total = run_peak + jnp.log(run_total)

        def value_step(tile_no, run_accum):
            scores, value_tile = tile_scores(tile_no)
            prob_bf = jnp.exp(scores - log_total[..., None]).astype(jnp.bfloat16)
            return run_accum + jnp.einsum(
                "kgqt,tkd->kgqd", prob_bf, value_tile, preferred_element_type=jnp.float32
            )

        run_accum = lax.fori_loop(
            0,
            tile_count,
            value_step,
            jnp.zeros((KEY_VALUE_HEADS, query_group_width, half_rows, HEAD_SIZE), jnp.float32),
        )
        context_half = jnp.transpose(run_accum, (2, 0, 1, 3)).reshape(half_rows, QW)
        return (context_half, log_total)

    query_flat = query_narrow.reshape(token_rows, QW)
    ctx_early, lse_early = attend(query_flat[:half_rows], early_block)
    ctx_late, lse_late = attend(query_flat[half_rows:], late_block)
    context_rows = jnp.concatenate([ctx_early, ctx_late], 0)
    context_bf = context_rows.astype(jnp.bfloat16)
    feature_cols, context_cols = (
        lax.all_to_all(normed, "wt", split_axis=1, concat_axis=0, tiled=True),
        lax.all_to_all(context_bf, "wt", split_axis=1, concat_axis=0, tiled=True),
    )
    mid_rows = x_rows + jnp.dot(context_bf, wo_b, preferred_element_type=jnp.float32)
    gain_two_full = gain_two.astype(jnp.float32)
    inv_rms_two = lax.rsqrt(jnp.mean(mid_rows * mid_rows, -1, keepdims=True) + norm_eps)
    normed_two = (mid_rows * inv_rms_two * gain_two_full).astype(jnp.bfloat16)
    cot_bf = cot_rows.astype(jnp.bfloat16)
    normed_group, cot_group = (
        lax.all_gather(normed_two, "wt", axis=0, tiled=True),
        lax.all_gather(cot_bf, "wt", axis=0, tiled=True),
    )
    gate_pre = inner_dot(normed_group, wg_own)
    up_pre = inner_dot(normed_group, wu_own)
    hidden_bf = hidden_units(gate_pre, up_pre)
    ff_sum = lax.psum_scatter(
        jnp.dot(hidden_bf, wd_own, preferred_element_type=jnp.float32),
        "wt",
        scatter_dimension=0,
        tiled=True,
    )
    d_hidden = inner_dot(cot_group, wd_own)
    d_gate, d_up = gate_terms(gate_pre, up_pre, d_hidden)
    ff_grads = jnp.concatenate(
        [
            outer_dot(d_gate, normed_group).astype(jnp.bfloat16),
            outer_dot(d_up, normed_group).astype(jnp.bfloat16),
            outer_dot(hidden_bf, cot_group).astype(jnp.bfloat16),
        ],
        0,
    )
    piece_len = moment1.shape[1]
    ff_rows = ff_grads.shape[0]
    taken = min(ff_rows, (piece_len // D + 2 + 16 + 15) // 16 * 16)
    first_rows = ff_first_row(n_ctx, piece_len, prefix, ff_rows, taken)
    ff_terms = lax.all_to_all(
        jnp.stack([ff_grads[row : row + taken] for row in first_rows]),
        "ctx",
        split_axis=0,
        concat_axis=0,
        tiled=True,
    )
    d_norm_two = lax.psum_scatter(
        jnp.dot(d_gate, wg_own, preferred_element_type=jnp.float32)
        + jnp.dot(d_up, wu_own, preferred_element_type=jnp.float32),
        "wt",
        scatter_dimension=0,
        tiled=True,
    )
    block_out = mid_rows + ff_sum
    grad_gain_two = jnp.sum(d_norm_two * mid_rows * inv_rms_two, 0)
    d_scaled_two = d_norm_two * gain_two_full
    d_mid = (
        cot_rows
        + inv_rms_two * d_scaled_two
        - mid_rows
        * (inv_rms_two * inv_rms_two * inv_rms_two)
        * jnp.mean(d_scaled_two * mid_rows, -1, keepdims=True)
    )
    d_mid_bf = d_mid.astype(jnp.bfloat16)
    context_gradient = inner_dot(d_mid_bf, wo_b)
    context_gradient_narrow = context_gradient.astype(jnp.bfloat16)
    delta_rows = jnp.sum(
        (context_gradient * context_rows).reshape(
            token_rows, KEY_VALUE_HEADS, query_group_width, HEAD_SIZE
        ),
        -1,
    )

    def attend_back(query_half, half_gradient, lse_half, delta_half, block_now, key_gradients):
        q_pos = query_positions(block_now)
        query_group = query_half.reshape(half_rows, KEY_VALUE_HEADS, query_group_width, HEAD_SIZE)
        group_gradient = half_gradient.reshape(
            half_rows, KEY_VALUE_HEADS, query_group_width, HEAD_SIZE
        )
        delta_t = jnp.transpose(delta_half, (1, 2, 0))[..., None]

        def tile_step(tile_no, state_carry):
            d_query, key_gradients = state_carry
            tile_start, key_block_tile, value_tile, k_pos = key_slice(tile_no)
            scores = score_scale * jnp.einsum(
                "qkgd,tkd->kgqt", query_group, key_block_tile, preferred_element_type=jnp.float32
            )
            visible = k_pos[None, :] <= q_pos[:, None]
            scores = jnp.where(visible, scores, -jnp.inf)
            prob_tile = jnp.where(visible, jnp.exp(scores - lse_half[..., None]), 0.0)
            prob_bf = prob_tile.astype(jnp.bfloat16)
            d_probs = jnp.einsum(
                "qkgd,tkd->kgqt", group_gradient, value_tile, preferred_element_type=jnp.float32
            )
            d_scores = (prob_tile * (d_probs - delta_t)).astype(jnp.bfloat16)
            d_query = d_query + score_scale * jnp.einsum(
                "kgqt,tkd->qkgd", d_scores, key_block_tile, preferred_element_type=jnp.float32
            )
            key_part = score_scale * jnp.einsum(
                "kgqt,qkgd->tkd", d_scores, query_group, preferred_element_type=jnp.float32
            )
            value_part = jnp.einsum(
                "kgqt,qkgd->tkd", prob_bf, group_gradient, preferred_element_type=jnp.float32
            )
            update = jnp.concatenate(
                [
                    key_part.reshape(key_tile, KEY_FEATURES),
                    value_part.reshape(key_tile, KEY_FEATURES),
                ],
                1,
            )
            current = lax.dynamic_slice_in_dim(key_gradients, tile_start, key_tile, 0)
            key_gradients = lax.dynamic_update_slice_in_dim(
                key_gradients, current + update, tile_start, 0
            )
            return (d_query, key_gradients)

        initial_state = (
            jnp.zeros((half_rows, KEY_VALUE_HEADS, query_group_width, HEAD_SIZE), jnp.float32),
            key_gradients,
        )
        return lax.fori_loop(0, tile_total(block_now), tile_step, initial_state)

    key_gradients = jnp.zeros((seq_len, 2 * KEY_FEATURES), jnp.float32)
    dq_early, key_gradients = attend_back(
        query_flat[:half_rows],
        context_gradient_narrow[:half_rows],
        lse_early,
        delta_rows[:half_rows],
        early_block,
        key_gradients,
    )
    dq_late, key_gradients = attend_back(
        query_flat[half_rows:],
        context_gradient_narrow[half_rows:],
        lse_late,
        delta_rows[half_rows:],
        late_block,
        key_gradients,
    )
    d_query_rot = jnp.concatenate([dq_early, dq_late], 0).reshape(
        token_rows, QUERY_HEADS, HEAD_SIZE
    )
    d_query = rotary_inverse(d_query_rot, cosine_table, sine_lookup).reshape(token_rows, QW)
    row_ids = jnp.arange(seq_len, dtype=jnp.int32)
    local_ids = row_ids % token_rows
    chosen = lookup(pairs, row_ids // token_rows)
    back_block = jnp.where(local_ids < half_rows, chosen, 2 * n_ctx - 1 - chosen)
    back_index = back_block * half_rows + local_ids % half_rows
    per_device = jnp.take(key_gradients, back_index, axis=0)
    owned_gradients = lax.psum_scatter(per_device, "ctx", scatter_dimension=0, tiled=True)
    key_gradient = rotary_inverse(
        owned_gradients[:, :KEY_FEATURES].reshape(token_rows, KEY_VALUE_HEADS, HEAD_SIZE),
        cosine_table,
        sine_lookup,
    ).reshape(token_rows, KEY_FEATURES)
    value_gradient = owned_gradients[:, KEY_FEATURES:]
    dq_bf = d_query.astype(jnp.bfloat16)
    dk_bf = key_gradient.astype(jnp.bfloat16)
    dv_bf = value_gradient.astype(jnp.bfloat16)
    d_norm = inner_dot(dq_bf, wq_b) + inner_dot(dk_bf, wk_b) + inner_dot(dv_bf, wv_b)
    grad_gain = jnp.sum(d_norm * x_rows * inv_rms, 0)
    d_scaled = d_norm * gain_full
    d_input = inv_rms * d_scaled - x_rows * (inv_rms * inv_rms * inv_rms) * jnp.mean(
        d_scaled * x_rows, -1, keepdims=True
    )
    input_grad = d_mid + d_input
    mid_group, query_grads, key_grads_group, value_grads_group = (
        lax.all_gather(d_mid_bf, "wt", axis=0, tiled=True),
        lax.all_gather(dq_bf, "wt", axis=0, tiled=True),
        lax.all_gather(dk_bf, "wt", axis=0, tiled=True),
        lax.all_gather(dv_bf, "wt", axis=0, tiled=True),
    )
    attn_grads = jnp.concatenate(
        [
            outer_dot(feature_cols, query_grads),
            outer_dot(feature_cols, key_grads_group),
            outer_dot(feature_cols, value_grads_group),
            outer_dot(context_cols, mid_group),
        ],
        1,
    ).astype(jnp.bfloat16)
    attn_part = attn_grads.shape[0] // n_ctx
    attn_terms = lax.all_to_all(
        attn_grads.reshape(n_ctx, attn_part, MATRIX_COLS),
        "ctx",
        split_axis=0,
        concat_axis=0,
        tiled=True,
    )
    attn_sum = lax.all_gather(
        jnp.sum(attn_terms.astype(jnp.float32), 0), "ctx", axis=0, tiled=True
    )
    vector_sums = lax.psum(
        jnp.concatenate(
            [
                grad_gain,
                jnp.sum(dq_bf.astype(jnp.float32), 0),
                jnp.sum(dk_bf.astype(jnp.float32), 0),
                jnp.sum(dv_bf.astype(jnp.float32), 0),
                grad_gain_two,
            ]
        ),
        ("ctx", "wt"),
    )
    small = []
    left = 0
    for full in (D, QW, KEY_FEATURES, KEY_FEATURES, D):
        small.append(
            lax.dynamic_slice_in_dim(vector_sums, left + wt_id * (full // n_wt), full // n_wt, 0)
        )
        left += full
    small, row_of_small = small_rows(small, [bounds[number] for number in vector_numbers])
    piece_start = ctx_id * piece_len
    flat_start = piece_start - D * lookup(jnp.array(first_rows, jnp.int32), ctx_id)
    own_row = piece_start // LANES // 8 * 8
    out_rows = (piece_len + LANES * 64 - 1) // (LANES * 64) * 64
    own_rows = lax.dynamic_slice_in_dim(flat_params, own_row, out_rows + 16, 0)
    place = jnp.stack(
        [
            flat_start // LANES,
            flat_start % LANES,
            piece_start // LANES - own_row,
            piece_start % LANES,
        ]
    ).astype(jnp.int32)
    grad_rows, param_rows = assemble(
        n_wt, small, row_of_small, attn_sum, ff_terms, own_rows, place, out_rows
    )
    param_grad = grad_rows.reshape(-1)[:piece_len].reshape(1, piece_len)
    own_params = param_rows.reshape(-1)[:piece_len].reshape(1, piece_len)
    decay = decay_mask(piece_start + jnp.arange(piece_len, dtype=jnp.int32), n_wt).reshape(
        1, piece_len
    )
    new_moment1 = beta_one * moment1 + (1.0 - beta_one) * param_grad
    new_moment2 = beta_two * moment2 + (1.0 - beta_two) * param_grad * param_grad
    m_hat = new_moment1 / (1.0 - beta_one**step_count)
    v_hat = new_moment2 / (1.0 - beta_two**step_count)
    new_params = own_params - learn_rate * (
        m_hat / (jnp.sqrt(v_hat) + adam_eps) + decay_rate * decay * own_params
    )
    return (
        block_out.reshape(1, token_rows, D),
        input_grad.reshape(1, token_rows, D),
        param_grad,
        new_params,
        new_moment1,
        new_moment2,
    )


def solution(mesh):
    in_specs = (
        P("wt", "ctx", None),
        P("wt", "ctx", None),
        P(),
        P("wt", "ctx"),
        P("wt", None),
        P("wt", "ctx"),
        P("wt", "ctx"),
    )
    out_specs = (
        P("wt", "ctx", None),
        P("wt", "ctx", None),
        P("wt", "ctx"),
        P("wt", "ctx"),
        P("wt", "ctx"),
        P("wt", "ctx"),
    )
    return jax.shard_map(body, mesh=mesh, in_specs=in_specs, out_specs=out_specs, check_vma=False)
```

```python
import math

import jax
import jax.numpy as jnp
from jax import lax
from jax.experimental import pallas as pl
from jax.experimental.pallas import tpu as pltpu
from jax.sharding import PartitionSpec as P

D = 896
QUERY_HEADS = 14
KEY_VALUE_HEADS = 2
HEAD_SIZE = 64
FF = 4864
QW = 896
KEY_FEATURES = 128


theta_base = 1000000.0
norm_eps = 1e-06
beta_one = 0.9
beta_two = 0.95
adam_eps = 1e-08
learn_rate = 0.02
decay_rate = 0.1
step_count = 10.0


def piece_shapes():
    return [
        (D, 0),
        (D, QW),
        (QW, 0),
        (D, KEY_FEATURES),
        (KEY_FEATURES, 0),
        (D, KEY_FEATURES),
        (KEY_FEATURES, 0),
        (QW, D),
        (D, 0),
        (FF, D),
        (FF, D),
        (FF, D),
    ]


def shard_bounds(parts):
    bounds = [0]
    for rows_full, cols in piece_shapes():
        length = rows_full // parts
        if cols > 0:
            length = length * cols
        bounds.append(bounds[-1] + length)
    return bounds


def unpack(rows_arr, parts, first, last):
    bounds = shard_bounds(parts)
    shapes = piece_shapes()
    count = rows_arr.shape[0]
    base = bounds[first]
    result = []
    for number in range(first, last):
        rows_full, cols = shapes[number]
        piece = rows_arr[:, bounds[number] - base : bounds[number + 1] - base]
        if cols > 0:
            result.append(piece.reshape(count * (rows_full // parts), cols))
        else:
            result.append(piece.reshape(-1))
    return result


def decay_mask(index_vec, parts):
    bounds = shard_bounds(parts)
    result = jnp.zeros(index_vec.shape, jnp.float32)
    for number in (1, 3, 5, 7, 9, 10, 11):
        inside = (index_vec >= bounds[number]) & (index_vec < bounds[number + 1])
        result = result + jnp.where(inside, 1.0, 0.0).astype(jnp.float32)
    return result


def rope_tables(position):
    freq_index = jnp.arange(HEAD_SIZE // 2, dtype=jnp.float32)
    inverse = jnp.exp(freq_index * (-2.0 * math.log(theta_base) / HEAD_SIZE))
    angles = position.astype(jnp.float32)[:, None] * inverse[None, :]
    cosine_table = jnp.cos(angles)
    sine_lookup = jnp.sin(angles)
    return (
        jnp.concatenate([cosine_table, cosine_table], 1),
        jnp.concatenate([sine_lookup, sine_lookup], 1),
    )


def rotary_apply(values, cosine_table, sine_lookup):
    top_half = values[..., HEAD_SIZE // 2 :]
    low_half = values[..., : HEAD_SIZE // 2]
    turned = jnp.concatenate([-top_half, low_half], -1)
    return values * cosine_table[:, None, :] + turned * sine_lookup[:, None, :]


def rotary_inverse(gradient, cosine_table, sine_lookup):
    scaled = gradient * sine_lookup[:, None, :]
    turned = jnp.concatenate([scaled[..., HEAD_SIZE // 2 :], -scaled[..., : HEAD_SIZE // 2]], -1)
    return gradient * cosine_table[:, None, :] + turned


def lookup(table, index_vec):
    slots = jnp.arange(table.shape[0], dtype=jnp.int32)
    return jnp.sum(jnp.where(index_vec[..., None] == slots, table, 0), -1)


def outer_dot(left, right):
    return lax.dot_general(
        left, right, (((0,), (0,)), ((), ())), preferred_element_type=jnp.float32
    )


def inner_dot(left, right):
    return lax.dot_general(
        left, right, (((1,), (1,)), ((), ())), preferred_element_type=jnp.float32
    )


def gate_terms(gate_pre, up_pre, d_hidden):
    sigmoid_gate = jax.nn.sigmoid(gate_pre)
    silu_gate = gate_pre * sigmoid_gate
    d_gate = (d_hidden * up_pre * sigmoid_gate * (1.0 + gate_pre * (1.0 - sigmoid_gate))).astype(
        jnp.bfloat16
    )
    d_up = (d_hidden * silu_gate).astype(jnp.bfloat16)
    return (d_gate, d_up)


def hidden_units(gate_pre, up_pre):
    return (gate_pre * jax.nn.sigmoid(gate_pre) * up_pre).astype(jnp.bfloat16)


LANES = 128
COLUMN_TILES = D // LANES
VMEM_BYTES = 56 * 1024 * 1024
MATRIX_COLS = QW + 2 * KEY_FEATURES + D


def big_pieces(parts):
    bounds = shard_bounds(parts)
    row_count = D // parts
    return [
        (bounds[1], row_count, COLUMN_TILES, 0),
        (bounds[3], row_count, 1, QW),
        (bounds[5], row_count, 1, QW + KEY_FEATURES),
        (bounds[7], row_count, COLUMN_TILES, QW + 2 * KEY_FEATURES),
    ]


def chunk_rows(rows):
    return 32 if rows % 32 == 0 else 16


def lane_ids(rows):
    return lax.broadcasted_iota(jnp.int32, (rows, LANES), 1)


def vector_rows(parts):
    bounds = shard_bounds(parts)
    return [
        (bounds[number] // LANES, (bounds[number + 1] - 1) // LANES + 1)
        for number in (0, 2, 4, 6, 8)
    ]


def unpack_kernel(parts, flat_ref, attn_ref, wg_ref, wu_ref, wd_ref, vector_ref, held):
    bounds = shard_bounds(parts)
    for number, (first_row, last_row) in enumerate(vector_rows(parts)):
        vector_ref[number, 0 : last_row - first_row, :] = flat_ref[first_row:last_row, :]

    def extract(base, rows, tiles, out_ref, column):
        step = chunk_rows(rows)
        flat_rows = step * tiles
        first, lane = base // LANES, base % LANES

        def chunk(number, carry):
            at = first + number * flat_rows
            if lane:
                low = pltpu.roll(flat_ref[pl.ds(at, flat_rows), :], LANES - lane, 1)
                high = pltpu.roll(flat_ref[pl.ds(at + 1, flat_rows), :], LANES - lane, 1)
                block = jnp.where(lane_ids(flat_rows) < LANES - lane, low, high)
            else:
                block = flat_ref[pl.ds(at, flat_rows), :]
            out_rows = pl.ds(pl.multiple_of(number * step, step), step)
            if tiles == 1:
                out_ref[out_rows, column : column + LANES] = block.astype(jnp.bfloat16)
            else:
                held[0:flat_rows, :] = block
                for tile in range(tiles):
                    part = held[pl.ds(tile, step, stride=tiles), :]
                    left = column + tile * LANES
                    out_ref[out_rows, left : left + LANES] = part.astype(jnp.bfloat16)
            return carry

        lax.fori_loop(0, rows // step, chunk, 0)

    for base, rows, tiles, column in big_pieces(parts):
        extract(base, rows, tiles, attn_ref, column)
    for number, out_ref in ((9, wg_ref), (10, wu_ref), (11, wd_ref)):
        extract(bounds[number], FF // parts, COLUMN_TILES, out_ref, 0)


def unpack_weights(flat_rows, parts):
    whole = pl.BlockSpec(memory_space=pltpu.VMEM)
    ff_rows = FF // parts
    return pl.pallas_call(
        lambda *refs: unpack_kernel(parts, *refs),
        out_shape=(
            jax.ShapeDtypeStruct((D // parts, MATRIX_COLS), jnp.bfloat16),
            jax.ShapeDtypeStruct((ff_rows, D), jnp.bfloat16),
            jax.ShapeDtypeStruct((ff_rows, D), jnp.bfloat16),
            jax.ShapeDtypeStruct((ff_rows, D), jnp.bfloat16),
            jax.ShapeDtypeStruct((5, 8, LANES), jnp.float32),
        ),
        in_specs=[whole],
        out_specs=(whole,) * 5,
        scratch_shapes=[pltpu.VMEM((32 * COLUMN_TILES, LANES), jnp.float32)],
        compiler_params=pltpu.CompilerParams(vmem_limit_bytes=VMEM_BYTES),
    )(flat_rows)


def small_rows(vectors, bases):
    rows = []
    where_rows = []
    for vector, base in zip(vectors, bases):
        lane = base % LANES
        end = lane + vector.shape[0]
        padded = jnp.pad(vector, (lane, -end % LANES)).reshape(-1, LANES)
        for extra in range(padded.shape[0]):
            where_rows.append(base // LANES + extra)
        rows.append(padded)
    stacked = jnp.concatenate(rows, 0)
    return jnp.pad(stacked, ((0, -stacked.shape[0] % 8), (0, 0))), where_rows


def ff_first_row(ctx_id, piece_len, prefix, total_rows, taken):
    rows = [
        min(max(0, (number * piece_len - prefix) // D // 16 * 16), total_rows - taken)
        for number in range(ctx_id)
    ]
    return rows


def assemble_kernel(
    parts, row_of_small, place_ref, small_ref, attn_ref, terms_ref, own_ref, grad_ref, param_ref,
    flat, held,
):
    senders, taken = terms_ref.shape[0], terms_ref.shape[1]
    prefix = shard_bounds(parts)[9]
    out_rows = grad_ref.shape[0]
    prefix_rows = prefix // LANES + 2
    flat[0:prefix_rows, :] = jnp.zeros((prefix_rows, LANES), jnp.float32)
    for number, row in enumerate(row_of_small):
        flat[row : row + 1, :] = flat[row : row + 1, :] + small_ref[number : number + 1, :]

    def insert(base, rows, tiles, load):
        step = 16
        flat_rows = step * tiles
        first, lane = base // LANES, base % LANES

        def chunk(number, carry):
            at = first + number * flat_rows
            for tile in range(tiles):
                part = load(pl.multiple_of(number * step, step), step, tile)
                if tiles == 1:
                    held[0:step, :] = part
                else:
                    held[pl.ds(tile, step, stride=tiles), :] = part
            block = held[0:flat_rows, :]
            if lane:
                block = pltpu.roll(block, lane, 1)
                ids = lane_ids(flat_rows)
                old = flat[pl.ds(at, flat_rows), :]
                flat[pl.ds(at, flat_rows), :] = jnp.where(ids < lane, old, block)
                old = flat[pl.ds(at + 1, flat_rows), :]
                flat[pl.ds(at + 1, flat_rows), :] = jnp.where(ids < lane, block, old)
            else:
                flat[pl.ds(at, flat_rows), :] = block
            return carry

        lax.fori_loop(0, rows // step, chunk, 0)

    def from_attn(column):
        def load(row, count, tile):
            left = column + tile * LANES
            return attn_ref[pl.ds(row, count), left : left + LANES]

        return load

    def from_terms(row, count, tile):
        columns = slice(tile * LANES, tile * LANES + LANES)
        total = terms_ref[0, pl.ds(row, count), columns].astype(jnp.float32)
        for sender in range(1, senders):
            total = total + terms_ref[sender, pl.ds(row, count), columns].astype(jnp.float32)
        return total

    for base, rows, tiles, column in big_pieces(parts):
        insert(base, rows, tiles, from_attn(column))
    insert(prefix, taken, COLUMN_TILES, from_terms)

    def shift(source, row_start, lane, out_ref):
        step = 64
        turn = (LANES - lane) % LANES

        def chunk(number, carry):
            at = row_start + number * step
            low = pltpu.roll(source[pl.ds(at, step), :], turn, 1)
            high = pltpu.roll(source[pl.ds(at + 1, step), :], turn, 1)
            out_ref[pl.ds(pl.multiple_of(number * step, step), step), :] = jnp.where(
                lane_ids(step) < LANES - lane, low, high
            )
            return carry

        lax.fori_loop(0, out_rows // step, chunk, 0)

    shift(flat, place_ref[0], place_ref[1], grad_ref)
    shift(own_ref, place_ref[2], place_ref[3], param_ref)


def assemble(parts, small, row_of_small, attn_sum, terms, own_rows, place, out_rows):
    whole = pl.BlockSpec(memory_space=pltpu.VMEM)
    prefix = shard_bounds(parts)[9]
    flat_rows = prefix // LANES + terms.shape[1] * COLUMN_TILES + out_rows // 8 * 8 + 80
    shape = jax.ShapeDtypeStruct((out_rows, LANES), jnp.float32)
    return pl.pallas_call(
        lambda *refs: assemble_kernel(parts, row_of_small, *refs),
        out_shape=(shape, shape),
        in_specs=[pl.BlockSpec(memory_space=pltpu.SMEM)] + [whole] * 4,
        out_specs=(whole, whole),
        scratch_shapes=[
            pltpu.VMEM((flat_rows, LANES), jnp.float32),
            pltpu.VMEM((16 * COLUMN_TILES, LANES), jnp.float32),
        ],
        compiler_params=pltpu.CompilerParams(vmem_limit_bytes=VMEM_BYTES),
    )(place, small, attn_sum, terms, own_rows)


MESH = pl.DeviceIdType.MESH


def exchange_kernel(
    n_ctx, n_wt, out_ref, back_ref, ff_ref, out_sum_ref, back_sum_ref, terms_ref,
    out_send, back_send, out_recv, back_recv, pair_recv, pair_sum,
    out_sems, back_sems, pair_sems, chip_sems,
):
    me_ctx, me_wt = lax.axis_index("ctx"), lax.axis_index("wt")
    core, chip = lax.rem(me_ctx, 2), lax.div(me_ctx, 2)
    chips = n_ctx // 2
    taken = terms_ref.shape[1]
    tokens = out_sum_ref.shape[0]
    sibling = chip * 2 + 1 - core

    def copy(source, target, sems, sent, landed, device):
        return pltpu.make_async_remote_copy(
            src_ref=source,
            dst_ref=target,
            send_sem=sems.at[0, sent],
            recv_sem=sems.at[1, landed],
            device_id=device,
            device_id_type=MESH,
        )

    wt_peers = [lax.rem(me_wt + step, n_wt) for step in range(1, n_wt)]
    chip_peers = [lax.rem(chip + step, chips) for step in range(1, chips)]
    barrier = pltpu.get_barrier_semaphore()
    partners = [(me_ctx, peer) for peer in wt_peers] + [(sibling, me_wt)]
    partners += [(peer * 2 + core, me_wt) for peer in chip_peers]
    for partner in partners:
        pl.semaphore_signal(barrier, inc=1, device_id=partner, device_id_type=MESH)
    pl.semaphore_wait(barrier, len(partners))

    def pair_copy(peer):
        source = ff_ref.at[peer * 2 + 1 - core]
        return copy(source, pair_recv.at[peer], pair_sems, peer, peer, (sibling, me_wt))

    def wt_copy(held, landing, sems, peer, slot):
        return copy(held.at[peer], landing.at[slot], sems, peer, slot, (me_ctx, peer))

    def chip_copy(peer, slot):
        device = (peer * 2 + core, me_wt)
        return copy(pair_sum.at[peer], terms_ref.at[slot], chip_sems, peer, slot, device)

    for peer in chip_peers + [chip]:
        pair_copy(peer).start()
    for source, held, landing, sems in (
        (back_ref, back_send, back_recv, back_sems),
        (out_ref, out_send, out_recv, out_sems),
    ):
        for peer in wt_peers:
            held[peer] = source[peer].astype(jnp.bfloat16)
            wt_copy(held, landing, sems, peer, me_wt).start()
    for peer in chip_peers + [chip]:
        pair_copy(peer).wait_recv()

        def add(number, carry):
            rows = pl.ds(pl.multiple_of(number * 32, 32), 32)
            total = ff_ref[peer * 2 + core, rows, :].astype(jnp.float32)
            total = total + pair_recv[peer, rows, :].astype(jnp.float32)
            pair_sum[peer, rows, :] = total.astype(jnp.bfloat16)
            return carry

        lax.fori_loop(0, taken // 32, add, 0)
        if peer is not chip:
            chip_copy(peer, chip).start()
    terms_ref[chip] = pair_sum[chip]
    for source, held, landing, sems, total_ref in (
        (back_ref, back_send, back_recv, back_sems, back_sum_ref),
        (out_ref, out_send, out_recv, out_sems, out_sum_ref),
    ):
        for peer in wt_peers:
            wt_copy(held, landing, sems, peer, peer).wait_recv()

        def total_step(number, carry):
            rows = pl.ds(pl.multiple_of(number * 16, 16), 16)
            total = source[me_wt, rows, :]
            for peer in wt_peers:
                total = total + landing[peer, rows, :].astype(jnp.float32)
            total_ref[rows, :] = total
            return carry

        lax.fori_loop(0, tokens // 16, total_step, 0)
    for peer in chip_peers:
        chip_copy(peer, peer).wait_recv()
    for peer in chip_peers + [chip]:
        pair_copy(peer).wait_send()
    for peer in chip_peers:
        chip_copy(peer, chip).wait_send()
    for held, landing, sems in (
        (back_send, back_recv, back_sems),
        (out_send, out_recv, out_sems),
    ):
        for peer in wt_peers:
            wt_copy(held, landing, sems, peer, me_wt).wait_send()


def exchange(out_terms, back_terms, ff_chunks):
    n_ctx, taken = ff_chunks.shape[0], ff_chunks.shape[1]
    n_wt, tokens = out_terms.shape[0], out_terms.shape[1]
    chips = n_ctx // 2
    whole = pl.BlockSpec(memory_space=pltpu.VMEM)
    rows = jax.ShapeDtypeStruct((tokens, D), jnp.float32)
    token_slots = pltpu.VMEM((n_wt, tokens, D), jnp.bfloat16)
    chip_slots = pltpu.VMEM((chips, taken, D), jnp.bfloat16)
    return pl.pallas_call(
        lambda *refs: exchange_kernel(n_ctx, n_wt, *refs),
        out_shape=(rows, rows, jax.ShapeDtypeStruct((chips, taken, D), jnp.bfloat16)),
        in_specs=[whole] * 3,
        out_specs=(whole,) * 3,
        scratch_shapes=[token_slots] * 4
        + [chip_slots] * 2
        + [pltpu.SemaphoreType.DMA((2, n_wt))] * 2
        + [pltpu.SemaphoreType.DMA((2, chips))] * 2,
        compiler_params=pltpu.CompilerParams(
            collective_id=1, has_side_effects=True, vmem_limit_bytes=VMEM_BYTES
        ),
    )(out_terms, back_terms, ff_chunks)


def body(block_in, cotangent, pairs, positions, params, moment1, moment2):
    n_ctx = lax.axis_size("ctx")
    n_wt = lax.axis_size("wt")
    token_rows = block_in.shape[1]
    half_rows = token_rows // 2
    seq_len = token_rows * n_ctx
    key_tile = min(512, seq_len)
    query_group_width = QUERY_HEADS // KEY_VALUE_HEADS
    score_scale = 1.0 / math.sqrt(HEAD_SIZE)
    ctx_id = lax.axis_index("ctx")
    wt_id = lax.axis_index("wt")
    x_rows = block_in[0]
    cot_rows = cotangent[0]
    bounds = shard_bounds(n_wt)
    prefix = bounds[9]
    shard_len = params.shape[1]
    flat_params = jnp.pad(params[0], (0, -shard_len % 1024 + 10240)).reshape(-1, LANES)
    attn_own, wg_own, wu_own, wd_own, vector_held = unpack_weights(flat_params, n_wt)
    vector_numbers = (0, 2, 4, 6, 8)
    vectors_own = vector_held.astype(jnp.bfloat16)
    attn_all = lax.all_gather(attn_own, "wt", axis=0, tiled=True)
    vectors_all = lax.all_gather(vectors_own, "wt", axis=0)
    wq_b = attn_all[:, :QW]
    wk_b = attn_all[:, QW : QW + KEY_FEATURES]
    wv_b = attn_all[:, QW + KEY_FEATURES : QW + 2 * KEY_FEATURES]
    wo_b = attn_all[:, QW + 2 * KEY_FEATURES :]
    vector_parts = []
    for place_no, number in enumerate(vector_numbers):
        lane = bounds[number] % LANES
        width = bounds[number + 1] - bounds[number]
        vector_parts.append(
            vectors_all[:, place_no].reshape(n_wt, 8 * LANES)[:, lane : lane + width].reshape(-1)
        )
    gain_b, bq_b, bk_b, bv_b, gain_two = vector_parts
    gain_full = gain_b.astype(jnp.float32)
    inv_rms = lax.rsqrt(jnp.mean(x_rows * x_rows, -1, keepdims=True) + norm_eps)
    normed = (x_rows * inv_rms * gain_full).astype(jnp.bfloat16)
    queries = jnp.dot(normed, wq_b, preferred_element_type=jnp.float32) + bq_b.astype(jnp.float32)
    key_projected = jnp.dot(normed, wk_b, preferred_element_type=jnp.float32) + bk_b.astype(
        jnp.float32
    )
    value_projected = jnp.dot(normed, wv_b, preferred_element_type=jnp.float32) + bv_b.astype(
        jnp.float32
    )
    cosine_table, sine_lookup = rope_tables(positions[0])
    query_narrow = rotary_apply(
        queries.reshape(token_rows, QUERY_HEADS, HEAD_SIZE), cosine_table, sine_lookup
    ).astype(jnp.bfloat16)
    key_narrow = rotary_apply(
        key_projected.reshape(token_rows, KEY_VALUE_HEADS, HEAD_SIZE), cosine_table, sine_lookup
    ).astype(jnp.bfloat16)
    value_narrow = value_projected.astype(jnp.bfloat16)
    own_kv = jnp.concatenate([key_narrow.reshape(token_rows, KEY_FEATURES), value_narrow], 1)
    all_kv = lax.all_gather(own_kv, "ctx", axis=0, tiled=True)
    block_ids = jnp.arange(2 * n_ctx, dtype=jnp.int32)
    target = jnp.where(block_ids < n_ctx, block_ids, 2 * n_ctx - 1 - block_ids)
    owner = jnp.sum(
        jnp.where(
            pairs[None, :] == target[:, None], jnp.arange(n_ctx, dtype=jnp.int32)[None, :], 0
        ),
        1,
    )
    late_side = (block_ids >= n_ctx).astype(jnp.int32)
    causal_ids = jnp.arange(seq_len, dtype=jnp.int32)
    block_of = causal_ids // half_rows
    source_row = (
        lookup(owner, block_of) * token_rows
        + lookup(late_side, block_of) * half_rows
        + causal_ids % half_rows
    )
    sorted_kv = jnp.take(all_kv, source_row, axis=0)
    early_block = lookup(pairs, ctx_id)
    late_block = 2 * n_ctx - 1 - early_block

    def query_positions(block_now):
        return block_now * half_rows + jnp.arange(half_rows, dtype=jnp.int32)

    def tile_total(block_now):
        return ((block_now + 1) * half_rows + key_tile - 1) // key_tile

    def key_slice(tile_no):
        tile_start = tile_no * key_tile
        key_value_tile = lax.dynamic_slice_in_dim(sorted_kv, tile_start, key_tile, 0)
        key_block_tile = key_value_tile[:, :KEY_FEATURES].reshape(
            key_tile, KEY_VALUE_HEADS, HEAD_SIZE
        )
        value_tile = key_value_tile[:, KEY_FEATURES:].reshape(key_tile, KEY_VALUE_HEADS, HEAD_SIZE)
        k_pos = tile_start + jnp.arange(key_tile, dtype=jnp.int32)
        return (tile_start, key_block_tile, value_tile, k_pos)

    def attend(query_half, block_now):
        q_pos = query_positions(block_now)
        query_group = query_half.reshape(half_rows, KEY_VALUE_HEADS, query_group_width, HEAD_SIZE)

        def tile_scores(tile_no):
            tile_start, key_block_tile, value_tile, k_pos = key_slice(tile_no)
            scores = score_scale * jnp.einsum(
                "qkgd,tkd->kgqt", query_group, key_block_tile, preferred_element_type=jnp.float32
            )
            visible = k_pos[None, :] <= q_pos[:, None]
            return (jnp.where(visible, scores, -jnp.inf), value_tile)

        def total_step(tile_no, state_carry):
            run_peak, run_total = state_carry
            scores, value_tile = tile_scores(tile_no)
            new_peak = jnp.maximum(run_peak, jnp.max(scores, -1))
            factor = jnp.exp(run_peak - new_peak)
            run_total = run_total * factor + jnp.sum(jnp.exp(scores - new_peak[..., None]), -1)
            return (new_peak, run_total)

        tile_count = tile_total(block_now)
        initial_state = (
            jnp.full((KEY_VALUE_HEADS, query_group_width, half_rows), -jnp.inf, jnp.float32),
            jnp.zeros((KEY_VALUE_HEADS, query_group_width, half_rows), jnp.float32),
        )
        run_peak, run_total = lax.fori_loop(0, tile_count, total_step, initial_state)
        log_total = run_peak + jnp.log(run_total)

        def value_step(tile_no, run_accum):
            scores, value_tile = tile_scores(tile_no)
            prob_bf = jnp.exp(scores - log_total[..., None]).astype(jnp.bfloat16)
            return run_accum + jnp.einsum(
                "kgqt,tkd->kgqd", prob_bf, value_tile, preferred_element_type=jnp.float32
            )

        run_accum = lax.fori_loop(
            0,
            tile_count,
            value_step,
            jnp.zeros((KEY_VALUE_HEADS, query_group_width, half_rows, HEAD_SIZE), jnp.float32),
        )
        context_half = jnp.transpose(run_accum, (2, 0, 1, 3)).reshape(half_rows, QW)
        return (context_half, log_total)

    query_flat = query_narrow.reshape(token_rows, QW)
    ctx_early, lse_early = attend(query_flat[:half_rows], early_block)
    ctx_late, lse_late = attend(query_flat[half_rows:], late_block)
    context_rows = jnp.concatenate([ctx_early, ctx_late], 0)
    context_bf = context_rows.astype(jnp.bfloat16)
    feature_cols, context_cols = (
        lax.all_to_all(normed, "wt", split_axis=1, concat_axis=0, tiled=True),
        lax.all_to_all(context_bf, "wt", split_axis=1, concat_axis=0, tiled=True),
    )
    mid_rows = x_rows + jnp.dot(context_bf, wo_b, preferred_element_type=jnp.float32)
    gain_two_full = gain_two.astype(jnp.float32)
    inv_rms_two = lax.rsqrt(jnp.mean(mid_rows * mid_rows, -1, keepdims=True) + norm_eps)
    normed_two = (mid_rows * inv_rms_two * gain_two_full).astype(jnp.bfloat16)
    cot_bf = cot_rows.astype(jnp.bfloat16)
    normed_group, cot_group = (
        lax.all_gather(normed_two, "wt", axis=0, tiled=True),
        lax.all_gather(cot_bf, "wt", axis=0, tiled=True),
    )
    gate_pre = inner_dot(normed_group, wg_own)
    up_pre = inner_dot(normed_group, wu_own)
    hidden_bf = hidden_units(gate_pre, up_pre)
    out_terms = jnp.dot(hidden_bf, wd_own, preferred_element_type=jnp.float32)
    d_hidden = inner_dot(cot_group, wd_own)
    d_gate, d_up = gate_terms(gate_pre, up_pre, d_hidden)
    ff_grads = jnp.concatenate(
        [
            outer_dot(d_gate, normed_group).astype(jnp.bfloat16),
            outer_dot(d_up, normed_group).astype(jnp.bfloat16),
            outer_dot(hidden_bf, cot_group).astype(jnp.bfloat16),
        ],
        0,
    )
    piece_len = moment1.shape[1]
    ff_rows = ff_grads.shape[0]
    taken = min(ff_rows, (piece_len // D + 2 + 16 + 31) // 32 * 32)
    first_rows = ff_first_row(n_ctx, piece_len, prefix, ff_rows, taken)
    back_terms = jnp.dot(d_gate, wg_own, preferred_element_type=jnp.float32) + jnp.dot(
        d_up, wu_own, preferred_element_type=jnp.float32
    )
    ff_sum, d_norm_two, ff_terms = exchange(
        out_terms.reshape(n_wt, token_rows, D),
        back_terms.reshape(n_wt, token_rows, D),
        jnp.stack([ff_grads[row : row + taken] for row in first_rows]),
    )
    block_out = mid_rows + ff_sum
    grad_gain_two = jnp.sum(d_norm_two * mid_rows * inv_rms_two, 0)
    d_scaled_two = d_norm_two * gain_two_full
    d_mid = (
        cot_rows
        + inv_rms_two * d_scaled_two
        - mid_rows
        * (inv_rms_two * inv_rms_two * inv_rms_two)
        * jnp.mean(d_scaled_two * mid_rows, -1, keepdims=True)
    )
    d_mid_bf = d_mid.astype(jnp.bfloat16)
    context_gradient = inner_dot(d_mid_bf, wo_b)
    context_gradient_narrow = context_gradient.astype(jnp.bfloat16)
    delta_rows = jnp.sum(
        (context_gradient * context_rows).reshape(
            token_rows, KEY_VALUE_HEADS, query_group_width, HEAD_SIZE
        ),
        -1,
    )

    def attend_back(query_half, half_gradient, lse_half, delta_half, block_now, key_gradients):
        q_pos = query_positions(block_now)
        query_group = query_half.reshape(half_rows, KEY_VALUE_HEADS, query_group_width, HEAD_SIZE)
        group_gradient = half_gradient.reshape(
            half_rows, KEY_VALUE_HEADS, query_group_width, HEAD_SIZE
        )
        delta_t = jnp.transpose(delta_half, (1, 2, 0))[..., None]

        def tile_step(tile_no, state_carry):
            d_query, key_gradients = state_carry
            tile_start, key_block_tile, value_tile, k_pos = key_slice(tile_no)
            scores = score_scale * jnp.einsum(
                "qkgd,tkd->kgqt", query_group, key_block_tile, preferred_element_type=jnp.float32
            )
            visible = k_pos[None, :] <= q_pos[:, None]
            scores = jnp.where(visible, scores, -jnp.inf)
            prob_tile = jnp.where(visible, jnp.exp(scores - lse_half[..., None]), 0.0)
            prob_bf = prob_tile.astype(jnp.bfloat16)
            d_probs = jnp.einsum(
                "qkgd,tkd->kgqt", group_gradient, value_tile, preferred_element_type=jnp.float32
            )
            d_scores = (prob_tile * (d_probs - delta_t)).astype(jnp.bfloat16)
            d_query = d_query + score_scale * jnp.einsum(
                "kgqt,tkd->qkgd", d_scores, key_block_tile, preferred_element_type=jnp.float32
            )
            key_part = score_scale * jnp.einsum(
                "kgqt,qkgd->tkd", d_scores, query_group, preferred_element_type=jnp.float32
            )
            value_part = jnp.einsum(
                "kgqt,qkgd->tkd", prob_bf, group_gradient, preferred_element_type=jnp.float32
            )
            update = jnp.concatenate(
                [
                    key_part.reshape(key_tile, KEY_FEATURES),
                    value_part.reshape(key_tile, KEY_FEATURES),
                ],
                1,
            )
            current = lax.dynamic_slice_in_dim(key_gradients, tile_start, key_tile, 0)
            key_gradients = lax.dynamic_update_slice_in_dim(
                key_gradients, current + update, tile_start, 0
            )
            return (d_query, key_gradients)

        initial_state = (
            jnp.zeros((half_rows, KEY_VALUE_HEADS, query_group_width, HEAD_SIZE), jnp.float32),
            key_gradients,
        )
        return lax.fori_loop(0, tile_total(block_now), tile_step, initial_state)

    key_gradients = jnp.zeros((seq_len, 2 * KEY_FEATURES), jnp.float32)
    dq_early, key_gradients = attend_back(
        query_flat[:half_rows],
        context_gradient_narrow[:half_rows],
        lse_early,
        delta_rows[:half_rows],
        early_block,
        key_gradients,
    )
    dq_late, key_gradients = attend_back(
        query_flat[half_rows:],
        context_gradient_narrow[half_rows:],
        lse_late,
        delta_rows[half_rows:],
        late_block,
        key_gradients,
    )
    d_query_rot = jnp.concatenate([dq_early, dq_late], 0).reshape(
        token_rows, QUERY_HEADS, HEAD_SIZE
    )
    d_query = rotary_inverse(d_query_rot, cosine_table, sine_lookup).reshape(token_rows, QW)
    row_ids = jnp.arange(seq_len, dtype=jnp.int32)
    local_ids = row_ids % token_rows
    chosen = lookup(pairs, row_ids // token_rows)
    back_block = jnp.where(local_ids < half_rows, chosen, 2 * n_ctx - 1 - chosen)
    back_index = back_block * half_rows + local_ids % half_rows
    per_device = jnp.take(key_gradients, back_index, axis=0)
    owned_gradients = lax.psum_scatter(per_device, "ctx", scatter_dimension=0, tiled=True)
    key_gradient = rotary_inverse(
        owned_gradients[:, :KEY_FEATURES].reshape(token_rows, KEY_VALUE_HEADS, HEAD_SIZE),
        cosine_table,
        sine_lookup,
    ).reshape(token_rows, KEY_FEATURES)
    value_gradient = owned_gradients[:, KEY_FEATURES:]
    dq_bf = d_query.astype(jnp.bfloat16)
    dk_bf = key_gradient.astype(jnp.bfloat16)
    dv_bf = value_gradient.astype(jnp.bfloat16)
    d_norm = inner_dot(dq_bf, wq_b) + inner_dot(dk_bf, wk_b) + inner_dot(dv_bf, wv_b)
    grad_gain = jnp.sum(d_norm * x_rows * inv_rms, 0)
    d_scaled = d_norm * gain_full
    d_input = inv_rms * d_scaled - x_rows * (inv_rms * inv_rms * inv_rms) * jnp.mean(
        d_scaled * x_rows, -1, keepdims=True
    )
    input_grad = d_mid + d_input
    mid_group, query_grads, key_grads_group, value_grads_group = (
        lax.all_gather(d_mid_bf, "wt", axis=0, tiled=True),
        lax.all_gather(dq_bf, "wt", axis=0, tiled=True),
        lax.all_gather(dk_bf, "wt", axis=0, tiled=True),
        lax.all_gather(dv_bf, "wt", axis=0, tiled=True),
    )
    attn_grads = jnp.concatenate(
        [
            outer_dot(feature_cols, query_grads),
            outer_dot(feature_cols, key_grads_group),
            outer_dot(feature_cols, value_grads_group),
            outer_dot(context_cols, mid_group),
        ],
        1,
    ).astype(jnp.bfloat16)
    attn_part = attn_grads.shape[0] // n_ctx
    attn_terms = lax.all_to_all(
        attn_grads.reshape(n_ctx, attn_part, MATRIX_COLS),
        "ctx",
        split_axis=0,
        concat_axis=0,
        tiled=True,
    )
    attn_sum = lax.all_gather(
        jnp.sum(attn_terms.astype(jnp.float32), 0), "ctx", axis=0, tiled=True
    )
    vector_sums = lax.psum(
        jnp.concatenate(
            [
                grad_gain,
                jnp.sum(dq_bf.astype(jnp.float32), 0),
                jnp.sum(dk_bf.astype(jnp.float32), 0),
                jnp.sum(dv_bf.astype(jnp.float32), 0),
                grad_gain_two,
            ]
        ),
        ("ctx", "wt"),
    )
    small = []
    left = 0
    for full in (D, QW, KEY_FEATURES, KEY_FEATURES, D):
        small.append(
            lax.dynamic_slice_in_dim(vector_sums, left + wt_id * (full // n_wt), full // n_wt, 0)
        )
        left += full
    small, row_of_small = small_rows(small, [bounds[number] for number in vector_numbers])
    piece_start = ctx_id * piece_len
    flat_start = piece_start - D * lookup(jnp.array(first_rows, jnp.int32), ctx_id)
    own_row = piece_start // LANES // 8 * 8
    out_rows = (piece_len + LANES * 64 - 1) // (LANES * 64) * 64
    own_rows = lax.dynamic_slice_in_dim(flat_params, own_row, out_rows + 16, 0)
    place = jnp.stack(
        [
            flat_start // LANES,
            flat_start % LANES,
            piece_start // LANES - own_row,
            piece_start % LANES,
        ]
    ).astype(jnp.int32)
    grad_rows, param_rows = assemble(
        n_wt, small, row_of_small, attn_sum, ff_terms, own_rows, place, out_rows
    )
    param_grad = grad_rows.reshape(1, -1)[:, :piece_len]
    own_params = param_rows.reshape(1, -1)[:, :piece_len]
    decay = decay_mask(piece_start + jnp.arange(piece_len, dtype=jnp.int32), n_wt).reshape(
        1, piece_len
    )
    new_moment1 = beta_one * moment1 + (1.0 - beta_one) * param_grad
    new_moment2 = beta_two * moment2 + (1.0 - beta_two) * param_grad * param_grad
    m_hat = new_moment1 / (1.0 - beta_one**step_count)
    v_hat = new_moment2 / (1.0 - beta_two**step_count)
    new_params = own_params - learn_rate * (
        m_hat / (jnp.sqrt(v_hat) + adam_eps) + decay_rate * decay * own_params
    )
    return (
        block_out.reshape(1, token_rows, D),
        input_grad.reshape(1, token_rows, D),
        param_grad,
        new_params,
        new_moment1,
        new_moment2,
    )


def solution(mesh):
    in_specs = (
        P("wt", "ctx", None),
        P("wt", "ctx", None),
        P(),
        P("wt", "ctx"),
        P("wt", None),
        P("wt", "ctx"),
        P("wt", "ctx"),
    )
    out_specs = (
        P("wt", "ctx", None),
        P("wt", "ctx", None),
        P("wt", "ctx"),
        P("wt", "ctx"),
        P("wt", "ctx"),
        P("wt", "ctx"),
    )
    return jax.shard_map(body, mesh=mesh, in_specs=in_specs, out_specs=out_specs, check_vma=False)
```

```python
import math

import jax
import jax.numpy as jnp
from jax import lax
from jax.experimental import pallas as pl
from jax.experimental.pallas import tpu as pltpu
from jax.sharding import PartitionSpec as P

D = 896
QUERY_HEADS = 14
KEY_VALUE_HEADS = 2
HEAD_SIZE = 64
FF = 4864
QW = 896
KEY_FEATURES = 128


theta_base = 1000000.0
norm_eps = 1e-06
beta_one = 0.9
beta_two = 0.95
adam_eps = 1e-08
learn_rate = 0.02
decay_rate = 0.1
step_count = 10.0


def piece_shapes():
    return [
        (D, 0),
        (D, QW),
        (QW, 0),
        (D, KEY_FEATURES),
        (KEY_FEATURES, 0),
        (D, KEY_FEATURES),
        (KEY_FEATURES, 0),
        (QW, D),
        (D, 0),
        (FF, D),
        (FF, D),
        (FF, D),
    ]


def shard_bounds(parts):
    bounds = [0]
    for rows_full, cols in piece_shapes():
        length = rows_full // parts
        if cols > 0:
            length = length * cols
        bounds.append(bounds[-1] + length)
    return bounds


def unpack(rows_arr, parts, first, last):
    bounds = shard_bounds(parts)
    shapes = piece_shapes()
    count = rows_arr.shape[0]
    base = bounds[first]
    result = []
    for number in range(first, last):
        rows_full, cols = shapes[number]
        piece = rows_arr[:, bounds[number] - base : bounds[number + 1] - base]
        if cols > 0:
            result.append(piece.reshape(count * (rows_full // parts), cols))
        else:
            result.append(piece.reshape(-1))
    return result


def decay_mask(index_vec, parts):
    bounds = shard_bounds(parts)
    result = jnp.zeros(index_vec.shape, jnp.float32)
    for number in (1, 3, 5, 7, 9, 10, 11):
        inside = (index_vec >= bounds[number]) & (index_vec < bounds[number + 1])
        result = result + jnp.where(inside, 1.0, 0.0).astype(jnp.float32)
    return result


def rope_tables(position):
    freq_index = jnp.arange(HEAD_SIZE // 2, dtype=jnp.float32)
    inverse = jnp.exp(freq_index * (-2.0 * math.log(theta_base) / HEAD_SIZE))
    angles = position.astype(jnp.float32)[:, None] * inverse[None, :]
    cosine_table = jnp.cos(angles)
    sine_lookup = jnp.sin(angles)
    return (
        jnp.concatenate([cosine_table, cosine_table], 1),
        jnp.concatenate([sine_lookup, sine_lookup], 1),
    )


def rotary_apply(values, cosine_table, sine_lookup):
    top_half = values[..., HEAD_SIZE // 2 :]
    low_half = values[..., : HEAD_SIZE // 2]
    turned = jnp.concatenate([-top_half, low_half], -1)
    return values * cosine_table[:, None, :] + turned * sine_lookup[:, None, :]


def rotary_inverse(gradient, cosine_table, sine_lookup):
    scaled = gradient * sine_lookup[:, None, :]
    turned = jnp.concatenate([scaled[..., HEAD_SIZE // 2 :], -scaled[..., : HEAD_SIZE // 2]], -1)
    return gradient * cosine_table[:, None, :] + turned


def lookup(table, index_vec):
    slots = jnp.arange(table.shape[0], dtype=jnp.int32)
    return jnp.sum(jnp.where(index_vec[..., None] == slots, table, 0), -1)


def outer_dot(left, right):
    return lax.dot_general(
        left, right, (((0,), (0,)), ((), ())), preferred_element_type=jnp.float32
    )


def inner_dot(left, right):
    return lax.dot_general(
        left, right, (((1,), (1,)), ((), ())), preferred_element_type=jnp.float32
    )


def gate_terms(gate_pre, up_pre, d_hidden):
    sigmoid_gate = jax.nn.sigmoid(gate_pre)
    silu_gate = gate_pre * sigmoid_gate
    d_gate = (d_hidden * up_pre * sigmoid_gate * (1.0 + gate_pre * (1.0 - sigmoid_gate))).astype(
        jnp.bfloat16
    )
    d_up = (d_hidden * silu_gate).astype(jnp.bfloat16)
    return (d_gate, d_up)


def hidden_units(gate_pre, up_pre):
    return (gate_pre * jax.nn.sigmoid(gate_pre) * up_pre).astype(jnp.bfloat16)


LANES = 128
MESH = pl.DeviceIdType.MESH
COLUMN_TILES = D // LANES
VMEM_BYTES = 56 * 1024 * 1024
MATRIX_COLS = QW + 2 * KEY_FEATURES + D


def big_pieces(parts):
    bounds = shard_bounds(parts)
    row_count = D // parts
    return [
        (bounds[1], row_count, COLUMN_TILES, 0),
        (bounds[3], row_count, 1, QW),
        (bounds[5], row_count, 1, QW + KEY_FEATURES),
        (bounds[7], row_count, COLUMN_TILES, QW + 2 * KEY_FEATURES),
    ]


def chunk_rows(rows):
    return 32 if rows % 32 == 0 else 16


def lane_ids(rows):
    return lax.broadcasted_iota(jnp.int32, (rows, LANES), 1)


def vector_rows(parts):
    bounds = shard_bounds(parts)
    return [
        (bounds[number] // LANES, (bounds[number + 1] - 1) // LANES + 1)
        for number in (0, 2, 4, 6, 8)
    ]


def remote(source, target, sent_sem, landed_sem, device):
    return pltpu.make_async_remote_copy(
        src_ref=source,
        dst_ref=target,
        send_sem=sent_sem,
        recv_sem=landed_sem,
        device_id=device,
        device_id_type=MESH,
    )


def meet(partners):
    barrier = pltpu.get_barrier_semaphore()
    for partner in partners:
        pl.semaphore_signal(barrier, inc=1, device_id=partner, device_id_type=MESH)
    pl.semaphore_wait(barrier, len(partners))


def unpack_kernel(
    parts, flat_ref, all_ref, vectors_ref, wg_ref, wu_ref, wd_ref,
    attn_ref, vector_ref, held, attn_sems, vector_sems, pair_sems, own_sems,
):
    bounds = shard_bounds(parts)
    me_ctx, me_wt = lax.axis_index("ctx"), lax.axis_index("wt")
    core = lax.rem(me_ctx, 2)
    sibling = me_ctx + 1 - 2 * core
    peers = [lax.rem(me_wt + step, parts) for step in range(1, parts)]
    half = MATRIX_COLS // 2
    mine = pl.ds(pl.multiple_of(core * half, half), half)
    theirs = pl.ds(pl.multiple_of((1 - core) * half, half), half)
    meet([(me_ctx, peer) for peer in peers] + [(sibling, me_wt)])

    def attn_copy(peer, slot):
        return remote(
            attn_ref.at[:, mine], all_ref.at[slot, :, mine],
            attn_sems.at[0, peer], attn_sems.at[1, slot], (me_ctx, peer),
        )

    def vector_copy(peer, slot):
        return remote(
            vector_ref, vectors_ref.at[slot],
            vector_sems.at[0, peer], vector_sems.at[1, slot], (me_ctx, peer),
        )

    def pair_copy(slot, columns):
        return remote(
            all_ref.at[slot, :, columns], all_ref.at[slot, :, columns],
            pair_sems.at[0, slot], pair_sems.at[1, slot], (sibling, me_wt),
        )

    for number, (first_row, last_row) in enumerate(vector_rows(parts)):
        vector_ref[number] = flat_ref[first_row : first_row + 16, :].astype(jnp.bfloat16)

    def extract(base, rows, tiles, out_ref, column):
        step = chunk_rows(rows)
        flat_rows = step * tiles
        first, lane = base // LANES, base % LANES

        def chunk(number, carry):
            at = first + number * flat_rows
            if lane:
                low = pltpu.roll(flat_ref[pl.ds(at, flat_rows), :], LANES - lane, 1)
                high = pltpu.roll(flat_ref[pl.ds(at + 1, flat_rows), :], LANES - lane, 1)
                block = jnp.where(lane_ids(flat_rows) < LANES - lane, low, high)
            else:
                block = flat_ref[pl.ds(at, flat_rows), :]
            out_rows = pl.ds(pl.multiple_of(number * step, step), step)
            if tiles == 1:
                out_ref[out_rows, column : column + LANES] = block.astype(jnp.bfloat16)
            else:
                held[0:flat_rows, :] = block
                for tile in range(tiles):
                    part = held[pl.ds(tile, step, stride=tiles), :]
                    left = column + tile * LANES
                    out_ref[out_rows, left : left + LANES] = part.astype(jnp.bfloat16)
            return carry

        lax.fori_loop(0, rows // step, chunk, 0)

    for base, rows, tiles, column in big_pieces(parts):
        extract(base, rows, tiles, attn_ref, column)
    for peer in peers:
        vector_copy(peer, me_wt).start()
        attn_copy(peer, me_wt).start()
    own_attn = pltpu.make_async_copy(attn_ref, all_ref.at[me_wt], own_sems.at[0])
    own_vector = pltpu.make_async_copy(vector_ref, vectors_ref.at[me_wt], own_sems.at[1])
    own_attn.start()
    own_vector.start()
    for number, out_ref in ((9, wg_ref), (10, wu_ref), (11, wd_ref)):
        extract(bounds[number], FF // parts, COLUMN_TILES, out_ref, 0)
    for peer in peers:
        attn_copy(peer, peer).wait_recv()
        pair_copy(peer, mine).start()
    for peer in peers:
        vector_copy(peer, peer).wait_recv()
        pair_copy(peer, theirs).wait_recv()
    own_attn.wait()
    own_vector.wait()
    for peer in peers:
        pair_copy(peer, mine).wait_send()
        attn_copy(peer, me_wt).wait_send()
        vector_copy(peer, me_wt).wait_send()


def unpack_weights(flat_rows, parts):
    whole = pl.BlockSpec(memory_space=pltpu.VMEM)
    anywhere = pl.BlockSpec(memory_space=pl.ANY)
    ff_shape = jax.ShapeDtypeStruct((FF // parts, D), jnp.bfloat16)
    return pl.pallas_call(
        lambda *refs: unpack_kernel(parts, *refs),
        out_shape=(
            jax.ShapeDtypeStruct((parts, D // parts, MATRIX_COLS), jnp.bfloat16),
            jax.ShapeDtypeStruct((parts, 5, 16, LANES), jnp.bfloat16),
            ff_shape,
            ff_shape,
            ff_shape,
        ),
        in_specs=[whole],
        out_specs=(anywhere, anywhere, whole, whole, whole),
        scratch_shapes=[
            pltpu.VMEM((D // parts, MATRIX_COLS), jnp.bfloat16),
            pltpu.VMEM((5, 16, LANES), jnp.bfloat16),
            pltpu.VMEM((32 * COLUMN_TILES, LANES), jnp.float32),
            pltpu.SemaphoreType.DMA((2, parts)),
            pltpu.SemaphoreType.DMA((2, parts)),
            pltpu.SemaphoreType.DMA((2, parts)),
            pltpu.SemaphoreType.DMA((2,)),
        ],
        compiler_params=pltpu.CompilerParams(
            collective_id=2, has_side_effects=True, vmem_limit_bytes=VMEM_BYTES
        ),
    )(flat_rows)


def gather_kernel(n_wt, count, *refs):
    sources, outs = refs[:count], refs[count : 2 * count]
    sems, own_sems = refs[2 * count :]
    me_ctx, me_wt = lax.axis_index("ctx"), lax.axis_index("wt")
    peers = [lax.rem(me_wt + step, n_wt) for step in range(1, n_wt)]
    meet([(me_ctx, peer) for peer in peers])

    def block(number, peer, slot):
        return remote(
            sources[number], outs[number].at[slot],
            sems.at[number, 0, peer], sems.at[number, 1, slot], (me_ctx, peer),
        )

    for peer in peers:
        for number in range(count):
            block(number, peer, me_wt).start()
    own = [
        pltpu.make_async_copy(sources[number], outs[number].at[me_wt], own_sems.at[number])
        for number in range(count)
    ]
    for copy in own:
        copy.start()
    for copy in own:
        copy.wait()
    for number in range(count):
        for peer in peers:
            block(number, peer, peer).wait_recv()
            block(number, peer, me_wt).wait_send()


def gather_wt(arrays, n_wt, collective_id):
    count = len(arrays)
    anywhere = pl.BlockSpec(memory_space=pl.ANY)
    gathered = pl.pallas_call(
        lambda *refs: gather_kernel(n_wt, count, *refs),
        out_shape=tuple(jax.ShapeDtypeStruct((n_wt,) + x.shape, x.dtype) for x in arrays),
        in_specs=[anywhere] * count,
        out_specs=(anywhere,) * count,
        scratch_shapes=[
            pltpu.SemaphoreType.DMA((count, 2, n_wt)),
            pltpu.SemaphoreType.DMA((count,)),
        ],
        compiler_params=pltpu.CompilerParams(collective_id=collective_id, has_side_effects=True),
    )(*arrays)
    return [x.reshape((-1,) + x.shape[2:]) for x in gathered]


def reduce_kernel(
    n_ctx, n_wt, owners, attn_ref, vector_ref, attn_sum_ref, vector_sum_ref,
    landed, partial, vector_landed, vector_partial, vector_terms,
    attn_sems, vector_sems, sum_sems, total_sems,
):
    me_ctx, me_wt = lax.axis_index("ctx"), lax.axis_index("wt")
    wt_peers = [lax.rem(me_wt + step, n_wt) for step in range(1, n_wt)]
    ctx_peers = [lax.rem(me_ctx + step, n_ctx) for step in range(1, n_ctx)]
    meet([(me_ctx, peer) for peer in wt_peers] + [(peer, me_wt) for peer in ctx_peers])

    def attn_copy(peer, slot):
        return remote(
            attn_ref.at[peer], landed.at[slot],
            attn_sems.at[0, peer], attn_sems.at[1, slot], (peer, me_wt),
        )

    def vector_copy(peer, slot):
        return remote(
            vector_ref, vector_landed.at[slot],
            vector_sems.at[0, peer], vector_sems.at[1, slot], (me_ctx, peer),
        )

    def sum_copy(owner, slot):
        return remote(
            partial, attn_sum_ref.at[slot],
            sum_sems.at[0, owner], sum_sems.at[1, slot], (owner, me_wt),
        )

    def total_copy(owner, slot):
        return remote(
            vector_partial, vector_terms.at[slot],
            total_sems.at[0, owner], total_sems.at[1, slot], (owner, me_wt),
        )

    for peer in wt_peers:
        vector_copy(peer, me_wt).start()
    for peer in ctx_peers:
        attn_copy(peer, me_ctx).start()
    vectors = vector_ref[...]
    for peer in wt_peers:
        vector_copy(peer, peer).wait_recv()
        vectors = vectors + vector_landed[peer]
    vector_partial[...] = vectors
    for owner in range(owners):

        @pl.when(me_ctx != owner)
        def _(owner=owner):
            total_copy(owner, me_ctx).start()

    total = attn_ref[me_ctx].astype(jnp.float32)
    for peer in ctx_peers:
        attn_copy(peer, peer).wait_recv()
        total = total + landed[peer].astype(jnp.float32)
    partial[...] = total
    for owner in range(owners):

        @pl.when(me_ctx != owner)
        def _(owner=owner):
            sum_copy(owner, me_ctx).start()

    attn_sum_ref[me_ctx] = total
    vector_sum_ref[...] = vectors

    @pl.when(me_ctx < owners)
    def _():
        summed = vectors
        for peer in ctx_peers:
            total_copy(0, peer).wait_recv()
            summed = summed + vector_terms[peer]
        vector_sum_ref[...] = summed
        for peer in ctx_peers:
            sum_copy(0, peer).wait_recv()

    for owner in range(owners):

        @pl.when(me_ctx != owner)
        def _(owner=owner):
            total_copy(owner, me_ctx).wait_send()
            sum_copy(owner, me_ctx).wait_send()

    for peer in wt_peers:
        vector_copy(peer, me_wt).wait_send()
    for peer in ctx_peers:
        attn_copy(peer, me_ctx).wait_send()


def reduce_attention(attn_grads, vectors, n_wt, owners):
    n_ctx = attn_grads.shape[0]
    whole = pl.BlockSpec(memory_space=pltpu.VMEM)
    block = attn_grads.shape[1:]
    return pl.pallas_call(
        lambda *refs: reduce_kernel(n_ctx, n_wt, owners, *refs),
        out_shape=(
            jax.ShapeDtypeStruct(attn_grads.shape, jnp.float32),
            jax.ShapeDtypeStruct(vectors.shape, jnp.float32),
        ),
        in_specs=[whole] * 2,
        out_specs=(whole, whole),
        scratch_shapes=[
            pltpu.VMEM(attn_grads.shape, jnp.bfloat16),
            pltpu.VMEM(block, jnp.float32),
            pltpu.VMEM((n_wt,) + vectors.shape, jnp.float32),
            pltpu.VMEM(vectors.shape, jnp.float32),
            pltpu.VMEM((n_ctx,) + vectors.shape, jnp.float32),
            pltpu.SemaphoreType.DMA((2, n_ctx)),
            pltpu.SemaphoreType.DMA((2, n_wt)),
            pltpu.SemaphoreType.DMA((2, n_ctx)),
            pltpu.SemaphoreType.DMA((2, n_ctx)),
        ],
        compiler_params=pltpu.CompilerParams(
            collective_id=3, has_side_effects=True, vmem_limit_bytes=VMEM_BYTES
        ),
    )(attn_grads, vectors)


def small_rows(vectors, bases):
    rows = []
    where_rows = []
    for vector, base in zip(vectors, bases):
        lane = base % LANES
        end = lane + vector.shape[0]
        padded = jnp.pad(vector, (lane, -end % LANES)).reshape(-1, LANES)
        for extra in range(padded.shape[0]):
            where_rows.append(base // LANES + extra)
        rows.append(padded)
    stacked = jnp.concatenate(rows, 0)
    return jnp.pad(stacked, ((0, -stacked.shape[0] % 8), (0, 0))), where_rows


def ff_first_row(ctx_id, piece_len, prefix, total_rows, taken):
    rows = [
        min(max(0, (number * piece_len - prefix) // D // 16 * 16), total_rows - taken)
        for number in range(ctx_id)
    ]
    return rows


def assemble_kernel(
    parts, row_of_small, place_ref, small_ref, attn_ref, terms_ref, own_ref, first_ref, second_ref,
    grad_ref, param_ref, new_first_ref, new_second_ref, flat, held,
):
    senders, taken = terms_ref.shape[0], terms_ref.shape[1]
    prefix = shard_bounds(parts)[9]
    out_rows = grad_ref.shape[0]
    prefix_rows = prefix // LANES + 2
    flat[0:prefix_rows, :] = jnp.zeros((prefix_rows, LANES), jnp.float32)
    for number, row in enumerate(row_of_small):
        flat[row : row + 1, :] = flat[row : row + 1, :] + small_ref[number : number + 1, :]

    def insert(base, rows, tiles, load):
        step = 16
        flat_rows = step * tiles
        first, lane = base // LANES, base % LANES

        def chunk(number, carry):
            at = first + number * flat_rows
            for tile in range(tiles):
                part = load(pl.multiple_of(number * step, step), step, tile)
                if tiles == 1:
                    held[0:step, :] = part
                else:
                    held[pl.ds(tile, step, stride=tiles), :] = part
            block = held[0:flat_rows, :]
            if lane:
                block = pltpu.roll(block, lane, 1)
                ids = lane_ids(flat_rows)
                old = flat[pl.ds(at, flat_rows), :]
                flat[pl.ds(at, flat_rows), :] = jnp.where(ids < lane, old, block)
                old = flat[pl.ds(at + 1, flat_rows), :]
                flat[pl.ds(at + 1, flat_rows), :] = jnp.where(ids < lane, block, old)
            else:
                flat[pl.ds(at, flat_rows), :] = block
            return carry

        lax.fori_loop(0, rows // step, chunk, 0)

    def from_attn(column):
        def load(row, count, tile):
            left = column + tile * LANES
            return attn_ref[pl.ds(row, count), left : left + LANES]

        return load

    def from_terms(row, count, tile):
        columns = slice(tile * LANES, tile * LANES + LANES)
        total = terms_ref[0, pl.ds(row, count), columns].astype(jnp.float32)
        for sender in range(1, senders):
            total = total + terms_ref[sender, pl.ds(row, count), columns].astype(jnp.float32)
        return total

    for base, rows, tiles, column in big_pieces(parts):
        insert(base, rows, tiles, from_attn(column))
    insert(prefix, taken, COLUMN_TILES, from_terms)

    def shifted(source, row_start, lane, at, step):
        turn = (LANES - lane) % LANES
        low = pltpu.roll(source[pl.ds(row_start + at, step), :], turn, 1)
        high = pltpu.roll(source[pl.ds(row_start + at + 1, step), :], turn, 1)
        return jnp.where(lane_ids(step) < LANES - lane, low, high)

    def update(number, carry):
        step = 64
        at = number * step
        rows = pl.ds(pl.multiple_of(at, step), step)
        grad = shifted(flat, place_ref[0], place_ref[1], at, step)
        own = shifted(own_ref, place_ref[2], place_ref[3], at, step)
        index_vec = (
            place_ref[4]
            + (lax.broadcasted_iota(jnp.int32, (step, LANES), 0) + at) * LANES
            + lane_ids(step)
        )
        decay = decay_mask(index_vec, parts)
        first = beta_one * first_ref[rows, :] + (1.0 - beta_one) * grad
        second = beta_two * second_ref[rows, :] + (1.0 - beta_two) * grad * grad
        m_hat = first / (1.0 - beta_one**step_count)
        v_hat = second / (1.0 - beta_two**step_count)
        grad_ref[rows, :] = grad
        new_first_ref[rows, :] = first
        new_second_ref[rows, :] = second
        param_ref[rows, :] = own - learn_rate * (
            m_hat / (jnp.sqrt(v_hat) + adam_eps) + decay_rate * decay * own
        )
        return carry

    lax.fori_loop(0, out_rows // 64, update, 0)


def assemble(parts, small, row_of_small, attn_sum, terms, own_rows, first, second, place):
    out_rows = first.shape[0]
    whole = pl.BlockSpec(memory_space=pltpu.VMEM)
    prefix = shard_bounds(parts)[9]
    flat_rows = prefix // LANES + terms.shape[1] * COLUMN_TILES + out_rows // 8 * 8 + 80
    shape = jax.ShapeDtypeStruct((out_rows, LANES), jnp.float32)
    return pl.pallas_call(
        lambda *refs: assemble_kernel(parts, row_of_small, *refs),
        out_shape=(shape,) * 4,
        in_specs=[pl.BlockSpec(memory_space=pltpu.SMEM)] + [whole] * 6,
        out_specs=(whole,) * 4,
        scratch_shapes=[
            pltpu.VMEM((flat_rows, LANES), jnp.float32),
            pltpu.VMEM((16 * COLUMN_TILES, LANES), jnp.float32),
        ],
        compiler_params=pltpu.CompilerParams(vmem_limit_bytes=VMEM_BYTES),
    )(place, small, attn_sum, terms, own_rows, first, second)


def exchange_kernel(
    n_ctx, n_wt, out_ref, back_ref, ff_ref, out_sum_ref, back_sum_ref, terms_ref,
    out_send, back_send, out_recv, back_recv, pair_recv, pair_sum,
    out_sems, back_sems, pair_sems, chip_sems,
):
    me_ctx, me_wt = lax.axis_index("ctx"), lax.axis_index("wt")
    core, chip = lax.rem(me_ctx, 2), lax.div(me_ctx, 2)
    chips = n_ctx // 2
    taken = terms_ref.shape[1]
    tokens = out_sum_ref.shape[0]
    sibling = chip * 2 + 1 - core

    def copy(source, target, sems, sent, landed, device):
        return pltpu.make_async_remote_copy(
            src_ref=source,
            dst_ref=target,
            send_sem=sems.at[0, sent],
            recv_sem=sems.at[1, landed],
            device_id=device,
            device_id_type=MESH,
        )

    wt_peers = [lax.rem(me_wt + step, n_wt) for step in range(1, n_wt)]
    chip_peers = [lax.rem(chip + step, chips) for step in range(1, chips)]
    barrier = pltpu.get_barrier_semaphore()
    partners = [(me_ctx, peer) for peer in wt_peers] + [(sibling, me_wt)]
    partners += [(peer * 2 + core, me_wt) for peer in chip_peers]
    for partner in partners:
        pl.semaphore_signal(barrier, inc=1, device_id=partner, device_id_type=MESH)
    pl.semaphore_wait(barrier, len(partners))

    def pair_copy(peer):
        source = ff_ref.at[peer * 2 + 1 - core]
        return copy(source, pair_recv.at[peer], pair_sems, peer, peer, (sibling, me_wt))

    def wt_copy(held, landing, sems, peer, slot):
        return copy(held.at[peer], landing.at[slot], sems, peer, slot, (me_ctx, peer))

    def chip_copy(peer, slot):
        device = (peer * 2 + core, me_wt)
        return copy(pair_sum.at[peer], terms_ref.at[slot], chip_sems, peer, slot, device)

    for peer in chip_peers + [chip]:
        pair_copy(peer).start()
    for source, held, landing, sems in (
        (back_ref, back_send, back_recv, back_sems),
        (out_ref, out_send, out_recv, out_sems),
    ):
        for peer in wt_peers:
            held[peer] = source[peer].astype(jnp.bfloat16)
            wt_copy(held, landing, sems, peer, me_wt).start()
    for peer in chip_peers + [chip]:
        pair_copy(peer).wait_recv()

        def add(number, carry):
            rows = pl.ds(pl.multiple_of(number * 32, 32), 32)
            total = ff_ref[peer * 2 + core, rows, :].astype(jnp.float32)
            total = total + pair_recv[peer, rows, :].astype(jnp.float32)
            pair_sum[peer, rows, :] = total.astype(jnp.bfloat16)
            return carry

        lax.fori_loop(0, taken // 32, add, 0)
        if peer is not chip:
            chip_copy(peer, chip).start()
    terms_ref[chip] = pair_sum[chip]
    for source, held, landing, sems, total_ref in (
        (back_ref, back_send, back_recv, back_sems, back_sum_ref),
        (out_ref, out_send, out_recv, out_sems, out_sum_ref),
    ):
        for peer in wt_peers:
            wt_copy(held, landing, sems, peer, peer).wait_recv()

        def total_step(number, carry):
            rows = pl.ds(pl.multiple_of(number * 16, 16), 16)
            total = source[me_wt, rows, :]
            for peer in wt_peers:
                total = total + landing[peer, rows, :].astype(jnp.float32)
            total_ref[rows, :] = total
            return carry

        lax.fori_loop(0, tokens // 16, total_step, 0)
    for peer in chip_peers:
        chip_copy(peer, peer).wait_recv()
    for peer in chip_peers + [chip]:
        pair_copy(peer).wait_send()
    for peer in chip_peers:
        chip_copy(peer, chip).wait_send()
    for held, landing, sems in (
        (back_send, back_recv, back_sems),
        (out_send, out_recv, out_sems),
    ):
        for peer in wt_peers:
            wt_copy(held, landing, sems, peer, me_wt).wait_send()


def exchange(out_terms, back_terms, ff_chunks):
    n_ctx, taken = ff_chunks.shape[0], ff_chunks.shape[1]
    n_wt, tokens = out_terms.shape[0], out_terms.shape[1]
    chips = n_ctx // 2
    whole = pl.BlockSpec(memory_space=pltpu.VMEM)
    rows = jax.ShapeDtypeStruct((tokens, D), jnp.float32)
    token_slots = pltpu.VMEM((n_wt, tokens, D), jnp.bfloat16)
    chip_slots = pltpu.VMEM((chips, taken, D), jnp.bfloat16)
    return pl.pallas_call(
        lambda *refs: exchange_kernel(n_ctx, n_wt, *refs),
        out_shape=(rows, rows, jax.ShapeDtypeStruct((chips, taken, D), jnp.bfloat16)),
        in_specs=[whole] * 3,
        out_specs=(whole,) * 3,
        scratch_shapes=[token_slots] * 4
        + [chip_slots] * 2
        + [pltpu.SemaphoreType.DMA((2, n_wt))] * 2
        + [pltpu.SemaphoreType.DMA((2, chips))] * 2,
        compiler_params=pltpu.CompilerParams(
            collective_id=1, has_side_effects=True, vmem_limit_bytes=VMEM_BYTES
        ),
    )(out_terms, back_terms, ff_chunks)


def body(block_in, cotangent, pairs, positions, params, moment1, moment2):
    n_ctx = lax.axis_size("ctx")
    n_wt = lax.axis_size("wt")
    token_rows = block_in.shape[1]
    half_rows = token_rows // 2
    seq_len = token_rows * n_ctx
    key_tile = min(512, seq_len)
    query_group_width = QUERY_HEADS // KEY_VALUE_HEADS
    score_scale = 1.0 / math.sqrt(HEAD_SIZE)
    ctx_id = lax.axis_index("ctx")
    wt_id = lax.axis_index("wt")
    x_rows = block_in[0]
    cot_rows = cotangent[0]
    bounds = shard_bounds(n_wt)
    prefix = bounds[9]
    shard_len = params.shape[1]
    flat_params = jnp.pad(params, ((0, 0), (0, -shard_len % 1024 + 10240))).reshape(-1, LANES)
    attn_all, vectors_all, wg_own, wu_own, wd_own = unpack_weights(flat_params, n_wt)
    attn_all = attn_all.reshape(D, MATRIX_COLS)
    vector_numbers = (0, 2, 4, 6, 8)
    wq_b = attn_all[:, :QW]
    wk_b = attn_all[:, QW : QW + KEY_FEATURES]
    wv_b = attn_all[:, QW + KEY_FEATURES : QW + 2 * KEY_FEATURES]
    wo_b = attn_all[:, QW + 2 * KEY_FEATURES :]
    vector_parts = []
    for place_no, number in enumerate(vector_numbers):
        lane = bounds[number] % LANES
        width = bounds[number + 1] - bounds[number]
        vector_parts.append(
            vectors_all[:, place_no].reshape(n_wt, 16 * LANES)[:, lane : lane + width].reshape(-1)
        )
    gain_b, bq_b, bk_b, bv_b, gain_two = vector_parts
    gain_full = gain_b.astype(jnp.float32)
    inv_rms = lax.rsqrt(jnp.mean(x_rows * x_rows, -1, keepdims=True) + norm_eps)
    normed = (x_rows * inv_rms * gain_full).astype(jnp.bfloat16)
    queries = jnp.dot(normed, wq_b, preferred_element_type=jnp.float32) + bq_b.astype(jnp.float32)
    key_projected = jnp.dot(normed, wk_b, preferred_element_type=jnp.float32) + bk_b.astype(
        jnp.float32
    )
    value_projected = jnp.dot(normed, wv_b, preferred_element_type=jnp.float32) + bv_b.astype(
        jnp.float32
    )
    cosine_table, sine_lookup = rope_tables(positions[0])
    query_narrow = rotary_apply(
        queries.reshape(token_rows, QUERY_HEADS, HEAD_SIZE), cosine_table, sine_lookup
    ).astype(jnp.bfloat16)
    key_narrow = rotary_apply(
        key_projected.reshape(token_rows, KEY_VALUE_HEADS, HEAD_SIZE), cosine_table, sine_lookup
    ).astype(jnp.bfloat16)
    value_narrow = value_projected.astype(jnp.bfloat16)
    own_kv = jnp.concatenate([key_narrow.reshape(token_rows, KEY_FEATURES), value_narrow], 1)
    all_kv = lax.all_gather(own_kv, "ctx", axis=0, tiled=True)
    block_ids = jnp.arange(2 * n_ctx, dtype=jnp.int32)
    target = jnp.where(block_ids < n_ctx, block_ids, 2 * n_ctx - 1 - block_ids)
    owner = jnp.sum(
        jnp.where(
            pairs[None, :] == target[:, None], jnp.arange(n_ctx, dtype=jnp.int32)[None, :], 0
        ),
        1,
    )
    late_side = (block_ids >= n_ctx).astype(jnp.int32)
    causal_ids = jnp.arange(seq_len, dtype=jnp.int32)
    block_of = causal_ids // half_rows
    source_row = (
        lookup(owner, block_of) * token_rows
        + lookup(late_side, block_of) * half_rows
        + causal_ids % half_rows
    )
    sorted_kv = jnp.take(all_kv, source_row, axis=0)
    early_block = lookup(pairs, ctx_id)
    late_block = 2 * n_ctx - 1 - early_block

    def query_positions(block_now):
        return block_now * half_rows + jnp.arange(half_rows, dtype=jnp.int32)

    def tile_total(block_now):
        return ((block_now + 1) * half_rows + key_tile - 1) // key_tile

    def key_slice(tile_no):
        tile_start = tile_no * key_tile
        key_value_tile = lax.dynamic_slice_in_dim(sorted_kv, tile_start, key_tile, 0)
        key_block_tile = key_value_tile[:, :KEY_FEATURES].reshape(
            key_tile, KEY_VALUE_HEADS, HEAD_SIZE
        )
        value_tile = key_value_tile[:, KEY_FEATURES:].reshape(key_tile, KEY_VALUE_HEADS, HEAD_SIZE)
        k_pos = tile_start + jnp.arange(key_tile, dtype=jnp.int32)
        return (tile_start, key_block_tile, value_tile, k_pos)

    def attend(query_half, block_now):
        q_pos = query_positions(block_now)
        query_group = query_half.reshape(half_rows, KEY_VALUE_HEADS, query_group_width, HEAD_SIZE)

        def tile_scores(tile_no):
            tile_start, key_block_tile, value_tile, k_pos = key_slice(tile_no)
            scores = score_scale * jnp.einsum(
                "qkgd,tkd->kgqt", query_group, key_block_tile, preferred_element_type=jnp.float32
            )
            visible = k_pos[None, :] <= q_pos[:, None]
            return (jnp.where(visible, scores, -jnp.inf), value_tile)

        def total_step(tile_no, state_carry):
            run_peak, run_total = state_carry
            scores, value_tile = tile_scores(tile_no)
            new_peak = jnp.maximum(run_peak, jnp.max(scores, -1))
            factor = jnp.exp(run_peak - new_peak)
            run_total = run_total * factor + jnp.sum(jnp.exp(scores - new_peak[..., None]), -1)
            return (new_peak, run_total)

        tile_count = tile_total(block_now)
        initial_state = (
            jnp.full((KEY_VALUE_HEADS, query_group_width, half_rows), -jnp.inf, jnp.float32),
            jnp.zeros((KEY_VALUE_HEADS, query_group_width, half_rows), jnp.float32),
        )
        run_peak, run_total = lax.fori_loop(0, tile_count, total_step, initial_state)
        log_total = run_peak + jnp.log(run_total)

        def value_step(tile_no, run_accum):
            scores, value_tile = tile_scores(tile_no)
            prob_bf = jnp.exp(scores - log_total[..., None]).astype(jnp.bfloat16)
            return run_accum + jnp.einsum(
                "kgqt,tkd->kgqd", prob_bf, value_tile, preferred_element_type=jnp.float32
            )

        run_accum = lax.fori_loop(
            0,
            tile_count,
            value_step,
            jnp.zeros((KEY_VALUE_HEADS, query_group_width, half_rows, HEAD_SIZE), jnp.float32),
        )
        context_half = jnp.transpose(run_accum, (2, 0, 1, 3)).reshape(half_rows, QW)
        return (context_half, log_total)

    query_flat = query_narrow.reshape(token_rows, QW)
    ctx_early, lse_early = attend(query_flat[:half_rows], early_block)
    ctx_late, lse_late = attend(query_flat[half_rows:], late_block)
    context_rows = jnp.concatenate([ctx_early, ctx_late], 0)
    context_bf = context_rows.astype(jnp.bfloat16)
    feature_cols, context_cols = (
        lax.all_to_all(normed, "wt", split_axis=1, concat_axis=0, tiled=True),
        lax.all_to_all(context_bf, "wt", split_axis=1, concat_axis=0, tiled=True),
    )
    mid_rows = x_rows + jnp.dot(context_bf, wo_b, preferred_element_type=jnp.float32)
    gain_two_full = gain_two.astype(jnp.float32)
    inv_rms_two = lax.rsqrt(jnp.mean(mid_rows * mid_rows, -1, keepdims=True) + norm_eps)
    normed_two = (mid_rows * inv_rms_two * gain_two_full).astype(jnp.bfloat16)
    cot_bf = cot_rows.astype(jnp.bfloat16)
    normed_group, cot_group = (
        lax.all_gather(normed_two, "wt", axis=0, tiled=True),
        lax.all_gather(cot_bf, "wt", axis=0, tiled=True),
    )
    gate_pre = inner_dot(normed_group, wg_own)
    up_pre = inner_dot(normed_group, wu_own)
    hidden_bf = hidden_units(gate_pre, up_pre)
    out_terms = jnp.dot(hidden_bf, wd_own, preferred_element_type=jnp.float32)
    d_hidden = inner_dot(cot_group, wd_own)
    d_gate, d_up = gate_terms(gate_pre, up_pre, d_hidden)
    ff_grads = jnp.concatenate(
        [
            outer_dot(d_gate, normed_group).astype(jnp.bfloat16),
            outer_dot(d_up, normed_group).astype(jnp.bfloat16),
            outer_dot(hidden_bf, cot_group).astype(jnp.bfloat16),
        ],
        0,
    )
    piece_len = moment1.shape[1]
    ff_rows = ff_grads.shape[0]
    taken = min(ff_rows, (piece_len // D + 2 + 16 + 31) // 32 * 32)
    first_rows = ff_first_row(n_ctx, piece_len, prefix, ff_rows, taken)
    back_terms = jnp.dot(d_gate, wg_own, preferred_element_type=jnp.float32) + jnp.dot(
        d_up, wu_own, preferred_element_type=jnp.float32
    )
    ff_sum, d_norm_two, ff_terms = exchange(
        out_terms.reshape(n_wt, token_rows, D),
        back_terms.reshape(n_wt, token_rows, D),
        jnp.stack([ff_grads[row : row + taken] for row in first_rows]),
    )
    block_out = mid_rows + ff_sum
    grad_gain_two = jnp.sum(d_norm_two * mid_rows * inv_rms_two, 0)
    d_scaled_two = d_norm_two * gain_two_full
    d_mid = (
        cot_rows
        + inv_rms_two * d_scaled_two
        - mid_rows
        * (inv_rms_two * inv_rms_two * inv_rms_two)
        * jnp.mean(d_scaled_two * mid_rows, -1, keepdims=True)
    )
    d_mid_bf = d_mid.astype(jnp.bfloat16)
    context_gradient = inner_dot(d_mid_bf, wo_b)
    context_gradient_narrow = context_gradient.astype(jnp.bfloat16)
    delta_rows = jnp.sum(
        (context_gradient * context_rows).reshape(
            token_rows, KEY_VALUE_HEADS, query_group_width, HEAD_SIZE
        ),
        -1,
    )

    def attend_back(query_half, half_gradient, lse_half, delta_half, block_now, key_gradients):
        q_pos = query_positions(block_now)
        query_group = query_half.reshape(half_rows, KEY_VALUE_HEADS, query_group_width, HEAD_SIZE)
        group_gradient = half_gradient.reshape(
            half_rows, KEY_VALUE_HEADS, query_group_width, HEAD_SIZE
        )
        delta_t = jnp.transpose(delta_half, (1, 2, 0))[..., None]

        def tile_step(tile_no, state_carry):
            d_query, key_gradients = state_carry
            tile_start, key_block_tile, value_tile, k_pos = key_slice(tile_no)
            scores = score_scale * jnp.einsum(
                "qkgd,tkd->kgqt", query_group, key_block_tile, preferred_element_type=jnp.float32
            )
            visible = k_pos[None, :] <= q_pos[:, None]
            scores = jnp.where(visible, scores, -jnp.inf)
            prob_tile = jnp.where(visible, jnp.exp(scores - lse_half[..., None]), 0.0)
            prob_bf = prob_tile.astype(jnp.bfloat16)
            d_probs = jnp.einsum(
                "qkgd,tkd->kgqt", group_gradient, value_tile, preferred_element_type=jnp.float32
            )
            d_scores = (prob_tile * (d_probs - delta_t)).astype(jnp.bfloat16)
            d_query = d_query + score_scale * jnp.einsum(
                "kgqt,tkd->qkgd", d_scores, key_block_tile, preferred_element_type=jnp.float32
            )
            key_part = score_scale * jnp.einsum(
                "kgqt,qkgd->tkd", d_scores, query_group, preferred_element_type=jnp.float32
            )
            value_part = jnp.einsum(
                "kgqt,qkgd->tkd", prob_bf, group_gradient, preferred_element_type=jnp.float32
            )
            update = jnp.concatenate(
                [
                    key_part.reshape(key_tile, KEY_FEATURES),
                    value_part.reshape(key_tile, KEY_FEATURES),
                ],
                1,
            )
            current = lax.dynamic_slice_in_dim(key_gradients, tile_start, key_tile, 0)
            key_gradients = lax.dynamic_update_slice_in_dim(
                key_gradients, current + update, tile_start, 0
            )
            return (d_query, key_gradients)

        initial_state = (
            jnp.zeros((half_rows, KEY_VALUE_HEADS, query_group_width, HEAD_SIZE), jnp.float32),
            key_gradients,
        )
        return lax.fori_loop(0, tile_total(block_now), tile_step, initial_state)

    key_gradients = jnp.zeros((seq_len, 2 * KEY_FEATURES), jnp.float32)
    dq_early, key_gradients = attend_back(
        query_flat[:half_rows],
        context_gradient_narrow[:half_rows],
        lse_early,
        delta_rows[:half_rows],
        early_block,
        key_gradients,
    )
    dq_late, key_gradients = attend_back(
        query_flat[half_rows:],
        context_gradient_narrow[half_rows:],
        lse_late,
        delta_rows[half_rows:],
        late_block,
        key_gradients,
    )
    d_query_rot = jnp.concatenate([dq_early, dq_late], 0).reshape(
        token_rows, QUERY_HEADS, HEAD_SIZE
    )
    d_query = rotary_inverse(d_query_rot, cosine_table, sine_lookup).reshape(token_rows, QW)
    row_ids = jnp.arange(seq_len, dtype=jnp.int32)
    local_ids = row_ids % token_rows
    chosen = lookup(pairs, row_ids // token_rows)
    back_block = jnp.where(local_ids < half_rows, chosen, 2 * n_ctx - 1 - chosen)
    back_index = back_block * half_rows + local_ids % half_rows
    per_device = jnp.take(key_gradients, back_index, axis=0)
    owned_gradients = lax.psum_scatter(per_device, "ctx", scatter_dimension=0, tiled=True)
    key_gradient = rotary_inverse(
        owned_gradients[:, :KEY_FEATURES].reshape(token_rows, KEY_VALUE_HEADS, HEAD_SIZE),
        cosine_table,
        sine_lookup,
    ).reshape(token_rows, KEY_FEATURES)
    value_gradient = owned_gradients[:, KEY_FEATURES:]
    dq_bf = d_query.astype(jnp.bfloat16)
    dk_bf = key_gradient.astype(jnp.bfloat16)
    dv_bf = value_gradient.astype(jnp.bfloat16)
    d_norm = inner_dot(dq_bf, wq_b) + inner_dot(dk_bf, wk_b) + inner_dot(dv_bf, wv_b)
    grad_gain = jnp.sum(d_norm * x_rows * inv_rms, 0)
    d_scaled = d_norm * gain_full
    d_input = inv_rms * d_scaled - x_rows * (inv_rms * inv_rms * inv_rms) * jnp.mean(
        d_scaled * x_rows, -1, keepdims=True
    )
    input_grad = d_mid + d_input
    mid_group, query_grads, key_value_grads = gather_wt(
        [d_mid_bf, dq_bf, jnp.concatenate([dk_bf, dv_bf], 1)], n_wt, 4
    )
    attn_grads = jnp.concatenate(
        [
            outer_dot(feature_cols, query_grads),
            outer_dot(feature_cols, key_value_grads),
            outer_dot(context_cols, mid_group),
        ],
        1,
    ).astype(jnp.bfloat16)
    attn_part = attn_grads.shape[0] // n_ctx
    vectors = jnp.concatenate(
        [
            grad_gain,
            jnp.sum(dq_bf.astype(jnp.float32), 0),
            jnp.sum(dk_bf.astype(jnp.float32), 0),
            jnp.sum(dv_bf.astype(jnp.float32), 0),
            grad_gain_two,
        ]
    )
    vectors = jnp.pad(vectors, (0, -vectors.shape[0] % 1024)).reshape(-1, LANES)
    attn_sum, vector_sums = reduce_attention(
        attn_grads.reshape(n_ctx, attn_part, MATRIX_COLS),
        vectors,
        n_wt,
        -(-prefix // piece_len),
    )
    attn_sum = attn_sum.reshape(n_ctx * attn_part, MATRIX_COLS)
    vector_sums = vector_sums.reshape(-1)
    small = []
    left = 0
    for full in (D, QW, KEY_FEATURES, KEY_FEATURES, D):
        small.append(
            lax.dynamic_slice_in_dim(vector_sums, left + wt_id * (full // n_wt), full // n_wt, 0)
        )
        left += full
    small, row_of_small = small_rows(small, [bounds[number] for number in vector_numbers])
    piece_start = ctx_id * piece_len
    flat_start = piece_start - D * lookup(jnp.array(first_rows, jnp.int32), ctx_id)
    own_row = piece_start // LANES // 8 * 8
    out_rows = (piece_len + LANES * 64 - 1) // (LANES * 64) * 64
    own_rows = lax.dynamic_slice_in_dim(flat_params, own_row, out_rows + 16, 0)
    place = jnp.stack(
        [
            flat_start // LANES,
            flat_start % LANES,
            piece_start // LANES - own_row,
            piece_start % LANES,
            piece_start,
        ]
    ).astype(jnp.int32)
    tail = ((0, 0), (0, out_rows * LANES - piece_len))
    updated = assemble(
        n_wt,
        small,
        row_of_small,
        attn_sum,
        ff_terms,
        own_rows,
        jnp.pad(moment1, tail).reshape(out_rows, LANES),
        jnp.pad(moment2, tail).reshape(out_rows, LANES),
        place,
    )
    param_grad, new_params, new_moment1, new_moment2 = [
        rows.reshape(1, -1)[:, :piece_len] for rows in updated
    ]
    return (
        block_out.reshape(1, token_rows, D),
        input_grad.reshape(1, token_rows, D),
        param_grad,
        new_params,
        new_moment1,
        new_moment2,
    )


def solution(mesh):
    in_specs = (
        P("wt", "ctx", None),
        P("wt", "ctx", None),
        P(),
        P("wt", "ctx"),
        P("wt", None),
        P("wt", "ctx"),
        P("wt", "ctx"),
    )
    out_specs = (
        P("wt", "ctx", None),
        P("wt", "ctx", None),
        P("wt", "ctx"),
        P("wt", "ctx"),
        P("wt", "ctx"),
        P("wt", "ctx"),
    )
    return jax.shard_map(body, mesh=mesh, in_specs=in_specs, out_specs=out_specs, check_vma=False)
```

```python
import math

import jax
import jax.numpy as jnp
from jax import lax
from jax.experimental import pallas as pl
from jax.experimental.pallas import tpu as pltpu
from jax.sharding import PartitionSpec as P

D = 896
QUERY_HEADS = 14
KEY_VALUE_HEADS = 2
HEAD_SIZE = 64
FF = 4864
QW = 896
KEY_FEATURES = 128


theta_base = 1000000.0
norm_eps = 1e-06
beta_one = 0.9
beta_two = 0.95
adam_eps = 1e-08
learn_rate = 0.02
decay_rate = 0.1
step_count = 10.0


def piece_shapes():
    return [
        (D, 0),
        (D, QW),
        (QW, 0),
        (D, KEY_FEATURES),
        (KEY_FEATURES, 0),
        (D, KEY_FEATURES),
        (KEY_FEATURES, 0),
        (QW, D),
        (D, 0),
        (FF, D),
        (FF, D),
        (FF, D),
    ]


def shard_bounds(parts):
    bounds = [0]
    for rows_full, cols in piece_shapes():
        length = rows_full // parts
        if cols > 0:
            length = length * cols
        bounds.append(bounds[-1] + length)
    return bounds


def unpack(rows_arr, parts, first, last):
    bounds = shard_bounds(parts)
    shapes = piece_shapes()
    count = rows_arr.shape[0]
    base = bounds[first]
    result = []
    for number in range(first, last):
        rows_full, cols = shapes[number]
        piece = rows_arr[:, bounds[number] - base : bounds[number + 1] - base]
        if cols > 0:
            result.append(piece.reshape(count * (rows_full // parts), cols))
        else:
            result.append(piece.reshape(-1))
    return result


def decay_mask(index_vec, parts):
    bounds = shard_bounds(parts)
    result = jnp.zeros(index_vec.shape, jnp.float32)
    for number in (1, 3, 5, 7, 9, 10, 11):
        inside = (index_vec >= bounds[number]) & (index_vec < bounds[number + 1])
        result = result + jnp.where(inside, 1.0, 0.0).astype(jnp.float32)
    return result


def rope_tables(position):
    freq_index = jnp.arange(HEAD_SIZE // 2, dtype=jnp.float32)
    inverse = jnp.exp(freq_index * (-2.0 * math.log(theta_base) / HEAD_SIZE))
    angles = position.astype(jnp.float32)[:, None] * inverse[None, :]
    cosine_table = jnp.cos(angles)
    sine_lookup = jnp.sin(angles)
    return (
        jnp.concatenate([cosine_table, cosine_table], 1),
        jnp.concatenate([sine_lookup, sine_lookup], 1),
    )


def rotary_apply(values, cosine_table, sine_lookup):
    top_half = values[..., HEAD_SIZE // 2 :]
    low_half = values[..., : HEAD_SIZE // 2]
    turned = jnp.concatenate([-top_half, low_half], -1)
    return values * cosine_table[:, None, :] + turned * sine_lookup[:, None, :]


def rotary_inverse(gradient, cosine_table, sine_lookup):
    scaled = gradient * sine_lookup[:, None, :]
    turned = jnp.concatenate([scaled[..., HEAD_SIZE // 2 :], -scaled[..., : HEAD_SIZE // 2]], -1)
    return gradient * cosine_table[:, None, :] + turned


def lookup(table, index_vec):
    slots = jnp.arange(table.shape[0], dtype=jnp.int32)
    return jnp.sum(jnp.where(index_vec[..., None] == slots, table, 0), -1)


def outer_dot(left, right):
    return lax.dot_general(
        left, right, (((0,), (0,)), ((), ())), preferred_element_type=jnp.float32
    )


def inner_dot(left, right):
    return lax.dot_general(
        left, right, (((1,), (1,)), ((), ())), preferred_element_type=jnp.float32
    )


def gate_terms(gate_pre, up_pre, d_hidden):
    sigmoid_gate = jax.nn.sigmoid(gate_pre)
    silu_gate = gate_pre * sigmoid_gate
    d_gate = (d_hidden * up_pre * sigmoid_gate * (1.0 + gate_pre * (1.0 - sigmoid_gate))).astype(
        jnp.bfloat16
    )
    d_up = (d_hidden * silu_gate).astype(jnp.bfloat16)
    return (d_gate, d_up)


def hidden_units(gate_pre, up_pre):
    return (gate_pre * jax.nn.sigmoid(gate_pre) * up_pre).astype(jnp.bfloat16)


LANES = 128
MESH = pl.DeviceIdType.MESH
COLUMN_TILES = D // LANES
VMEM_BYTES = 56 * 1024 * 1024
MATRIX_COLS = QW + 2 * KEY_FEATURES + D


def big_pieces(parts):
    bounds = shard_bounds(parts)
    row_count = D // parts
    return [
        (bounds[1], row_count, COLUMN_TILES, 0),
        (bounds[3], row_count, 1, QW),
        (bounds[5], row_count, 1, QW + KEY_FEATURES),
        (bounds[7], row_count, COLUMN_TILES, QW + 2 * KEY_FEATURES),
    ]


def chunk_rows(rows):
    return 32 if rows % 32 == 0 else 16


def lane_ids(rows):
    return lax.broadcasted_iota(jnp.int32, (rows, LANES), 1)


def vector_rows(parts):
    bounds = shard_bounds(parts)
    return [
        (bounds[number] // LANES, (bounds[number + 1] - 1) // LANES + 1)
        for number in (0, 2, 4, 6, 8)
    ]


def remote(source, target, sent_sem, landed_sem, device):
    return pltpu.make_async_remote_copy(
        src_ref=source,
        dst_ref=target,
        send_sem=sent_sem,
        recv_sem=landed_sem,
        device_id=device,
        device_id_type=MESH,
    )


def meet(partners):
    barrier = pltpu.get_barrier_semaphore()
    for partner in partners:
        pl.semaphore_signal(barrier, inc=1, device_id=partner, device_id_type=MESH)
    pl.semaphore_wait(barrier, len(partners))


def unpack_kernel(
    parts, flat_ref, all_ref, vectors_ref, wg_ref, wu_ref, wd_ref,
    attn_ref, vector_ref, held, attn_sems, vector_sems, pair_sems, own_sems,
):
    bounds = shard_bounds(parts)
    me_ctx, me_wt = lax.axis_index("ctx"), lax.axis_index("wt")
    core = lax.rem(me_ctx, 2)
    sibling = me_ctx + 1 - 2 * core
    peers = [lax.rem(me_wt + step, parts) for step in range(1, parts)]
    half = MATRIX_COLS // 2
    mine = pl.ds(pl.multiple_of(core * half, half), half)
    theirs = pl.ds(pl.multiple_of((1 - core) * half, half), half)
    meet([(me_ctx, peer) for peer in peers] + [(sibling, me_wt)])

    def attn_copy(peer, slot):
        return remote(
            attn_ref.at[:, mine], all_ref.at[slot, :, mine],
            attn_sems.at[0, peer], attn_sems.at[1, slot], (me_ctx, peer),
        )

    def vector_copy(peer, slot):
        return remote(
            vector_ref, vectors_ref.at[slot],
            vector_sems.at[0, peer], vector_sems.at[1, slot], (me_ctx, peer),
        )

    def pair_copy(slot, columns):
        return remote(
            all_ref.at[slot, :, columns], all_ref.at[slot, :, columns],
            pair_sems.at[0, slot], pair_sems.at[1, slot], (sibling, me_wt),
        )

    for number, (first_row, last_row) in enumerate(vector_rows(parts)):
        vector_ref[number] = flat_ref[first_row : first_row + 16, :].astype(jnp.bfloat16)

    def extract(base, rows, tiles, out_ref, column):
        step = chunk_rows(rows)
        flat_rows = step * tiles
        first, lane = base // LANES, base % LANES

        def chunk(number, carry):
            at = first + number * flat_rows
            if lane:
                low = pltpu.roll(flat_ref[pl.ds(at, flat_rows), :], LANES - lane, 1)
                high = pltpu.roll(flat_ref[pl.ds(at + 1, flat_rows), :], LANES - lane, 1)
                block = jnp.where(lane_ids(flat_rows) < LANES - lane, low, high)
            else:
                block = flat_ref[pl.ds(at, flat_rows), :]
            out_rows = pl.ds(pl.multiple_of(number * step, step), step)
            if tiles == 1:
                out_ref[out_rows, column : column + LANES] = block.astype(jnp.bfloat16)
            else:
                held[0:flat_rows, :] = block
                for tile in range(tiles):
                    part = held[pl.ds(tile, step, stride=tiles), :]
                    left = column + tile * LANES
                    out_ref[out_rows, left : left + LANES] = part.astype(jnp.bfloat16)
            return carry

        lax.fori_loop(0, rows // step, chunk, 0)

    for base, rows, tiles, column in big_pieces(parts):
        extract(base, rows, tiles, attn_ref, column)
    for peer in peers:
        vector_copy(peer, me_wt).start()
        attn_copy(peer, me_wt).start()
    own_attn = pltpu.make_async_copy(attn_ref, all_ref.at[me_wt], own_sems.at[0])
    own_vector = pltpu.make_async_copy(vector_ref, vectors_ref.at[me_wt], own_sems.at[1])
    own_attn.start()
    own_vector.start()
    for number, out_ref in ((9, wg_ref), (10, wu_ref), (11, wd_ref)):
        extract(bounds[number], FF // parts, COLUMN_TILES, out_ref, 0)
    for peer in peers:
        attn_copy(peer, peer).wait_recv()
        pair_copy(peer, mine).start()
    for peer in peers:
        vector_copy(peer, peer).wait_recv()
        pair_copy(peer, theirs).wait_recv()
    own_attn.wait()
    own_vector.wait()
    for peer in peers:
        pair_copy(peer, mine).wait_send()
        attn_copy(peer, me_wt).wait_send()
        vector_copy(peer, me_wt).wait_send()


def unpack_weights(flat_rows, parts):
    whole = pl.BlockSpec(memory_space=pltpu.VMEM)
    anywhere = pl.BlockSpec(memory_space=pl.ANY)
    ff_shape = jax.ShapeDtypeStruct((FF // parts, D), jnp.bfloat16)
    return pl.pallas_call(
        lambda *refs: unpack_kernel(parts, *refs),
        out_shape=(
            jax.ShapeDtypeStruct((parts, D // parts, MATRIX_COLS), jnp.bfloat16),
            jax.ShapeDtypeStruct((parts, 5, 16, LANES), jnp.bfloat16),
            ff_shape,
            ff_shape,
            ff_shape,
        ),
        in_specs=[whole],
        out_specs=(anywhere, anywhere, whole, whole, whole),
        scratch_shapes=[
            pltpu.VMEM((D // parts, MATRIX_COLS), jnp.bfloat16),
            pltpu.VMEM((5, 16, LANES), jnp.bfloat16),
            pltpu.VMEM((32 * COLUMN_TILES, LANES), jnp.float32),
            pltpu.SemaphoreType.DMA((2, parts)),
            pltpu.SemaphoreType.DMA((2, parts)),
            pltpu.SemaphoreType.DMA((2, parts)),
            pltpu.SemaphoreType.DMA((2,)),
        ],
        compiler_params=pltpu.CompilerParams(
            collective_id=2, has_side_effects=True, vmem_limit_bytes=VMEM_BYTES
        ),
    )(flat_rows)


def gather_kernel(n_wt, count, scattered, *refs):
    sources, outs = refs[:count], refs[count : 2 * count]
    sems, own_sems = refs[2 * count :]
    me_ctx, me_wt = lax.axis_index("ctx"), lax.axis_index("wt")
    peers = [lax.rem(me_wt + step, n_wt) for step in range(1, n_wt)]
    meet([(me_ctx, peer) for peer in peers])

    def part(number, peer):
        return sources[number].at[peer] if number < scattered else sources[number]

    def block(number, peer, slot):
        return remote(
            part(number, peer), outs[number].at[slot],
            sems.at[number, 0, peer], sems.at[number, 1, slot], (me_ctx, peer),
        )

    for peer in peers:
        for number in range(count):
            block(number, peer, me_wt).start()
    own = [
        pltpu.make_async_copy(part(number, me_wt), outs[number].at[me_wt], own_sems.at[number])
        for number in range(count)
    ]
    for copy in own:
        copy.start()
    for copy in own:
        copy.wait()
    for number in range(count):
        for peer in peers:
            block(number, peer, peer).wait_recv()
            block(number, peer, me_wt).wait_send()


def gather_wt(arrays, n_wt, scattered, collective_id):
    count = len(arrays)
    blocks = [x.shape[1:] if k < scattered else x.shape for k, x in enumerate(arrays)]
    anywhere = pl.BlockSpec(memory_space=pl.ANY)
    gathered = pl.pallas_call(
        lambda *refs: gather_kernel(n_wt, count, scattered, *refs),
        out_shape=tuple(
            jax.ShapeDtypeStruct((n_wt,) + block, x.dtype) for block, x in zip(blocks, arrays)
        ),
        in_specs=[anywhere] * count,
        out_specs=(anywhere,) * count,
        scratch_shapes=[
            pltpu.SemaphoreType.DMA((count, 2, n_wt)),
            pltpu.SemaphoreType.DMA((count,)),
        ],
        compiler_params=pltpu.CompilerParams(collective_id=collective_id, has_side_effects=True),
    )(*arrays)
    return [x.reshape((-1,) + x.shape[2:]) for x in gathered]


def reduce_kernel(
    n_ctx, n_wt, owners, attn_ref, vector_ref, attn_sum_ref, vector_sum_ref,
    landed, partial, vector_landed, vector_partial, vector_terms,
    attn_sems, vector_sems, sum_sems, total_sems,
):
    me_ctx, me_wt = lax.axis_index("ctx"), lax.axis_index("wt")
    wt_peers = [lax.rem(me_wt + step, n_wt) for step in range(1, n_wt)]
    ctx_peers = [lax.rem(me_ctx + step, n_ctx) for step in range(1, n_ctx)]
    meet([(me_ctx, peer) for peer in wt_peers] + [(peer, me_wt) for peer in ctx_peers])

    def attn_copy(peer, slot):
        return remote(
            attn_ref.at[peer], landed.at[slot],
            attn_sems.at[0, peer], attn_sems.at[1, slot], (peer, me_wt),
        )

    def vector_copy(peer, slot):
        return remote(
            vector_ref, vector_landed.at[slot],
            vector_sems.at[0, peer], vector_sems.at[1, slot], (me_ctx, peer),
        )

    def sum_copy(owner, slot):
        return remote(
            partial, attn_sum_ref.at[slot],
            sum_sems.at[0, owner], sum_sems.at[1, slot], (owner, me_wt),
        )

    def total_copy(owner, slot):
        return remote(
            vector_partial, vector_terms.at[slot],
            total_sems.at[0, owner], total_sems.at[1, slot], (owner, me_wt),
        )

    for peer in wt_peers:
        vector_copy(peer, me_wt).start()
    for peer in ctx_peers:
        attn_copy(peer, me_ctx).start()
    vectors = vector_ref[...]
    for peer in wt_peers:
        vector_copy(peer, peer).wait_recv()
        vectors = vectors + vector_landed[peer]
    vector_partial[...] = vectors
    for owner in range(owners):

        @pl.when(me_ctx != owner)
        def _(owner=owner):
            total_copy(owner, me_ctx).start()

    total = attn_ref[me_ctx].astype(jnp.float32)
    for peer in ctx_peers:
        attn_copy(peer, peer).wait_recv()
        total = total + landed[peer].astype(jnp.float32)
    partial[...] = total
    for owner in range(owners):

        @pl.when(me_ctx != owner)
        def _(owner=owner):
            sum_copy(owner, me_ctx).start()

    attn_sum_ref[me_ctx] = total
    vector_sum_ref[...] = vectors

    @pl.when(me_ctx < owners)
    def _():
        summed = vectors
        for peer in ctx_peers:
            total_copy(0, peer).wait_recv()
            summed = summed + vector_terms[peer]
        vector_sum_ref[...] = summed
        for peer in ctx_peers:
            sum_copy(0, peer).wait_recv()

    for owner in range(owners):

        @pl.when(me_ctx != owner)
        def _(owner=owner):
            total_copy(owner, me_ctx).wait_send()
            sum_copy(owner, me_ctx).wait_send()

    for peer in wt_peers:
        vector_copy(peer, me_wt).wait_send()
    for peer in ctx_peers:
        attn_copy(peer, me_ctx).wait_send()


def reduce_attention(attn_grads, vectors, n_wt, owners):
    n_ctx = attn_grads.shape[0]
    whole = pl.BlockSpec(memory_space=pltpu.VMEM)
    block = attn_grads.shape[1:]
    return pl.pallas_call(
        lambda *refs: reduce_kernel(n_ctx, n_wt, owners, *refs),
        out_shape=(
            jax.ShapeDtypeStruct(attn_grads.shape, jnp.float32),
            jax.ShapeDtypeStruct(vectors.shape, jnp.float32),
        ),
        in_specs=[whole] * 2,
        out_specs=(whole, whole),
        scratch_shapes=[
            pltpu.VMEM(attn_grads.shape, jnp.bfloat16),
            pltpu.VMEM(block, jnp.float32),
            pltpu.VMEM((n_wt,) + vectors.shape, jnp.float32),
            pltpu.VMEM(vectors.shape, jnp.float32),
            pltpu.VMEM((n_ctx,) + vectors.shape, jnp.float32),
            pltpu.SemaphoreType.DMA((2, n_ctx)),
            pltpu.SemaphoreType.DMA((2, n_wt)),
            pltpu.SemaphoreType.DMA((2, n_ctx)),
            pltpu.SemaphoreType.DMA((2, n_ctx)),
        ],
        compiler_params=pltpu.CompilerParams(
            collective_id=3, has_side_effects=True, vmem_limit_bytes=VMEM_BYTES
        ),
    )(attn_grads, vectors)


def small_rows(vectors, bases):
    rows = []
    where_rows = []
    for vector, base in zip(vectors, bases):
        lane = base % LANES
        end = lane + vector.shape[0]
        padded = jnp.pad(vector, (lane, -end % LANES)).reshape(-1, LANES)
        for extra in range(padded.shape[0]):
            where_rows.append(base // LANES + extra)
        rows.append(padded)
    stacked = jnp.concatenate(rows, 0)
    return jnp.pad(stacked, ((0, -stacked.shape[0] % 8), (0, 0))), where_rows


def ff_first_row(ctx_id, piece_len, prefix, total_rows, taken):
    rows = [
        min(max(0, (number * piece_len - prefix) // D // 16 * 16), total_rows - taken)
        for number in range(ctx_id)
    ]
    return rows


def assemble_kernel(
    parts, row_of_small, place_ref, small_ref, attn_ref, terms_ref, own_ref, first_ref, second_ref,
    grad_ref, param_ref, new_first_ref, new_second_ref, flat, held,
):
    senders, taken = terms_ref.shape[0], terms_ref.shape[1]
    prefix = shard_bounds(parts)[9]
    out_rows = grad_ref.shape[0]
    prefix_rows = prefix // LANES + 2
    flat[0:prefix_rows, :] = jnp.zeros((prefix_rows, LANES), jnp.float32)
    for number, row in enumerate(row_of_small):
        flat[row : row + 1, :] = flat[row : row + 1, :] + small_ref[number : number + 1, :]

    def insert(base, rows, tiles, load):
        step = 16
        flat_rows = step * tiles
        first, lane = base // LANES, base % LANES

        def chunk(number, carry):
            at = first + number * flat_rows
            for tile in range(tiles):
                part = load(pl.multiple_of(number * step, step), step, tile)
                if tiles == 1:
                    held[0:step, :] = part
                else:
                    held[pl.ds(tile, step, stride=tiles), :] = part
            block = held[0:flat_rows, :]
            if lane:
                block = pltpu.roll(block, lane, 1)
                ids = lane_ids(flat_rows)
                old = flat[pl.ds(at, flat_rows), :]
                flat[pl.ds(at, flat_rows), :] = jnp.where(ids < lane, old, block)
                old = flat[pl.ds(at + 1, flat_rows), :]
                flat[pl.ds(at + 1, flat_rows), :] = jnp.where(ids < lane, block, old)
            else:
                flat[pl.ds(at, flat_rows), :] = block
            return carry

        lax.fori_loop(0, rows // step, chunk, 0)

    def from_attn(column):
        def load(row, count, tile):
            left = column + tile * LANES
            return attn_ref[pl.ds(row, count), left : left + LANES]

        return load

    def from_terms(row, count, tile):
        columns = slice(tile * LANES, tile * LANES + LANES)
        total = terms_ref[0, pl.ds(row, count), columns].astype(jnp.float32)
        for sender in range(1, senders):
            total = total + terms_ref[sender, pl.ds(row, count), columns].astype(jnp.float32)
        return total

    for base, rows, tiles, column in big_pieces(parts):
        insert(base, rows, tiles, from_attn(column))
    insert(prefix, taken, COLUMN_TILES, from_terms)

    def shifted(source, row_start, lane, at, step):
        turn = (LANES - lane) % LANES
        low = pltpu.roll(source[pl.ds(row_start + at, step), :], turn, 1)
        high = pltpu.roll(source[pl.ds(row_start + at + 1, step), :], turn, 1)
        return jnp.where(lane_ids(step) < LANES - lane, low, high)

    def update(number, carry):
        step = 64
        at = number * step
        rows = pl.ds(pl.multiple_of(at, step), step)
        grad = shifted(flat, place_ref[0], place_ref[1], at, step)
        own = shifted(own_ref, place_ref[2], place_ref[3], at, step)
        index_vec = (
            place_ref[4]
            + (lax.broadcasted_iota(jnp.int32, (step, LANES), 0) + at) * LANES
            + lane_ids(step)
        )
        decay = decay_mask(index_vec, parts)
        first = beta_one * first_ref[rows, :] + (1.0 - beta_one) * grad
        second = beta_two * second_ref[rows, :] + (1.0 - beta_two) * grad * grad
        m_hat = first / (1.0 - beta_one**step_count)
        v_hat = second / (1.0 - beta_two**step_count)
        grad_ref[rows, :] = grad
        new_first_ref[rows, :] = first
        new_second_ref[rows, :] = second
        param_ref[rows, :] = own - learn_rate * (
            m_hat / (jnp.sqrt(v_hat) + adam_eps) + decay_rate * decay * own
        )
        return carry

    lax.fori_loop(0, out_rows // 64, update, 0)


def assemble(parts, small, row_of_small, attn_sum, terms, own_rows, first, second, place):
    out_rows = first.shape[0]
    whole = pl.BlockSpec(memory_space=pltpu.VMEM)
    prefix = shard_bounds(parts)[9]
    flat_rows = prefix // LANES + terms.shape[1] * COLUMN_TILES + out_rows // 8 * 8 + 80
    shape = jax.ShapeDtypeStruct((out_rows, LANES), jnp.float32)
    return pl.pallas_call(
        lambda *refs: assemble_kernel(parts, row_of_small, *refs),
        out_shape=(shape,) * 4,
        in_specs=[pl.BlockSpec(memory_space=pltpu.SMEM)] + [whole] * 6,
        out_specs=(whole,) * 4,
        scratch_shapes=[
            pltpu.VMEM((flat_rows, LANES), jnp.float32),
            pltpu.VMEM((16 * COLUMN_TILES, LANES), jnp.float32),
        ],
        compiler_params=pltpu.CompilerParams(vmem_limit_bytes=VMEM_BYTES),
    )(place, small, attn_sum, terms, own_rows, first, second)


def exchange_kernel(
    n_ctx, n_wt, out_ref, back_ref, ff_ref, out_sum_ref, back_sum_ref, terms_ref,
    out_send, back_send, out_recv, back_recv, pair_recv, pair_sum,
    out_sems, back_sems, pair_sems, chip_sems,
):
    me_ctx, me_wt = lax.axis_index("ctx"), lax.axis_index("wt")
    core, chip = lax.rem(me_ctx, 2), lax.div(me_ctx, 2)
    chips = n_ctx // 2
    taken = terms_ref.shape[1]
    tokens = out_sum_ref.shape[0]
    sibling = chip * 2 + 1 - core

    def copy(source, target, sems, sent, landed, device):
        return pltpu.make_async_remote_copy(
            src_ref=source,
            dst_ref=target,
            send_sem=sems.at[0, sent],
            recv_sem=sems.at[1, landed],
            device_id=device,
            device_id_type=MESH,
        )

    wt_peers = [lax.rem(me_wt + step, n_wt) for step in range(1, n_wt)]
    chip_peers = [lax.rem(chip + step, chips) for step in range(1, chips)]
    barrier = pltpu.get_barrier_semaphore()
    partners = [(me_ctx, peer) for peer in wt_peers] + [(sibling, me_wt)]
    partners += [(peer * 2 + core, me_wt) for peer in chip_peers]
    for partner in partners:
        pl.semaphore_signal(barrier, inc=1, device_id=partner, device_id_type=MESH)
    pl.semaphore_wait(barrier, len(partners))

    def pair_copy(peer):
        source = ff_ref.at[peer * 2 + 1 - core]
        return copy(source, pair_recv.at[peer], pair_sems, peer, peer, (sibling, me_wt))

    def wt_copy(held, landing, sems, peer, slot):
        return copy(held.at[peer], landing.at[slot], sems, peer, slot, (me_ctx, peer))

    def chip_copy(peer, slot):
        device = (peer * 2 + core, me_wt)
        return copy(pair_sum.at[peer], terms_ref.at[slot], chip_sems, peer, slot, device)

    for peer in chip_peers + [chip]:
        pair_copy(peer).start()
    for source, held, landing, sems in (
        (back_ref, back_send, back_recv, back_sems),
        (out_ref, out_send, out_recv, out_sems),
    ):
        for peer in wt_peers:
            held[peer] = source[peer].astype(jnp.bfloat16)
            wt_copy(held, landing, sems, peer, me_wt).start()
    for peer in chip_peers + [chip]:
        pair_copy(peer).wait_recv()

        def add(number, carry):
            rows = pl.ds(pl.multiple_of(number * 32, 32), 32)
            total = ff_ref[peer * 2 + core, rows, :].astype(jnp.float32)
            total = total + pair_recv[peer, rows, :].astype(jnp.float32)
            pair_sum[peer, rows, :] = total.astype(jnp.bfloat16)
            return carry

        lax.fori_loop(0, taken // 32, add, 0)
        if peer is not chip:
            chip_copy(peer, chip).start()
    terms_ref[chip] = pair_sum[chip]
    for source, held, landing, sems, total_ref in (
        (back_ref, back_send, back_recv, back_sems, back_sum_ref),
        (out_ref, out_send, out_recv, out_sems, out_sum_ref),
    ):
        for peer in wt_peers:
            wt_copy(held, landing, sems, peer, peer).wait_recv()

        def total_step(number, carry):
            rows = pl.ds(pl.multiple_of(number * 16, 16), 16)
            total = source[me_wt, rows, :]
            for peer in wt_peers:
                total = total + landing[peer, rows, :].astype(jnp.float32)
            total_ref[rows, :] = total
            return carry

        lax.fori_loop(0, tokens // 16, total_step, 0)
    for peer in chip_peers:
        chip_copy(peer, peer).wait_recv()
    for peer in chip_peers + [chip]:
        pair_copy(peer).wait_send()
    for peer in chip_peers:
        chip_copy(peer, chip).wait_send()
    for held, landing, sems in (
        (back_send, back_recv, back_sems),
        (out_send, out_recv, out_sems),
    ):
        for peer in wt_peers:
            wt_copy(held, landing, sems, peer, me_wt).wait_send()


def exchange(out_terms, back_terms, ff_chunks):
    n_ctx, taken = ff_chunks.shape[0], ff_chunks.shape[1]
    n_wt, tokens = out_terms.shape[0], out_terms.shape[1]
    chips = n_ctx // 2
    whole = pl.BlockSpec(memory_space=pltpu.VMEM)
    rows = jax.ShapeDtypeStruct((tokens, D), jnp.float32)
    token_slots = pltpu.VMEM((n_wt, tokens, D), jnp.bfloat16)
    chip_slots = pltpu.VMEM((chips, taken, D), jnp.bfloat16)
    return pl.pallas_call(
        lambda *refs: exchange_kernel(n_ctx, n_wt, *refs),
        out_shape=(rows, rows, jax.ShapeDtypeStruct((chips, taken, D), jnp.bfloat16)),
        in_specs=[whole] * 3,
        out_specs=(whole,) * 3,
        scratch_shapes=[token_slots] * 4
        + [chip_slots] * 2
        + [pltpu.SemaphoreType.DMA((2, n_wt))] * 2
        + [pltpu.SemaphoreType.DMA((2, chips))] * 2,
        compiler_params=pltpu.CompilerParams(
            collective_id=1, has_side_effects=True, vmem_limit_bytes=VMEM_BYTES
        ),
    )(out_terms, back_terms, ff_chunks)


def body(block_in, cotangent, pairs, positions, params, moment1, moment2):
    n_ctx = lax.axis_size("ctx")
    n_wt = lax.axis_size("wt")
    token_rows = block_in.shape[1]
    half_rows = token_rows // 2
    seq_len = token_rows * n_ctx
    key_tile = min(512, seq_len)
    query_group_width = QUERY_HEADS // KEY_VALUE_HEADS
    score_scale = 1.0 / math.sqrt(HEAD_SIZE)
    ctx_id = lax.axis_index("ctx")
    wt_id = lax.axis_index("wt")
    x_rows = block_in[0]
    cot_rows = cotangent[0]
    bounds = shard_bounds(n_wt)
    prefix = bounds[9]
    shard_len = params.shape[1]
    flat_params = jnp.pad(params, ((0, 0), (0, -shard_len % 1024 + 10240))).reshape(-1, LANES)
    attn_all, vectors_all, wg_own, wu_own, wd_own = unpack_weights(flat_params, n_wt)
    attn_all = attn_all.reshape(D, MATRIX_COLS)
    vector_numbers = (0, 2, 4, 6, 8)
    wq_b = attn_all[:, :QW]
    wk_b = attn_all[:, QW : QW + KEY_FEATURES]
    wv_b = attn_all[:, QW + KEY_FEATURES : QW + 2 * KEY_FEATURES]
    wo_b = attn_all[:, QW + 2 * KEY_FEATURES :]
    vector_parts = []
    for place_no, number in enumerate(vector_numbers):
        lane = bounds[number] % LANES
        width = bounds[number + 1] - bounds[number]
        vector_parts.append(
            vectors_all[:, place_no].reshape(n_wt, 16 * LANES)[:, lane : lane + width].reshape(-1)
        )
    gain_b, bq_b, bk_b, bv_b, gain_two = vector_parts
    gain_full = gain_b.astype(jnp.float32)
    inv_rms = lax.rsqrt(jnp.mean(x_rows * x_rows, -1, keepdims=True) + norm_eps)
    normed = (x_rows * inv_rms * gain_full).astype(jnp.bfloat16)
    queries = jnp.dot(normed, wq_b, preferred_element_type=jnp.float32) + bq_b.astype(jnp.float32)
    key_projected = jnp.dot(normed, wk_b, preferred_element_type=jnp.float32) + bk_b.astype(
        jnp.float32
    )
    value_projected = jnp.dot(normed, wv_b, preferred_element_type=jnp.float32) + bv_b.astype(
        jnp.float32
    )
    cosine_table, sine_lookup = rope_tables(positions[0])
    query_narrow = rotary_apply(
        queries.reshape(token_rows, QUERY_HEADS, HEAD_SIZE), cosine_table, sine_lookup
    ).astype(jnp.bfloat16)
    key_narrow = rotary_apply(
        key_projected.reshape(token_rows, KEY_VALUE_HEADS, HEAD_SIZE), cosine_table, sine_lookup
    ).astype(jnp.bfloat16)
    value_narrow = value_projected.astype(jnp.bfloat16)
    own_kv = jnp.concatenate([key_narrow.reshape(token_rows, KEY_FEATURES), value_narrow], 1)
    all_kv = lax.all_gather(own_kv, "ctx", axis=0, tiled=True)
    block_ids = jnp.arange(2 * n_ctx, dtype=jnp.int32)
    target = jnp.where(block_ids < n_ctx, block_ids, 2 * n_ctx - 1 - block_ids)
    owner = jnp.sum(
        jnp.where(
            pairs[None, :] == target[:, None], jnp.arange(n_ctx, dtype=jnp.int32)[None, :], 0
        ),
        1,
    )
    late_side = (block_ids >= n_ctx).astype(jnp.int32)
    causal_ids = jnp.arange(seq_len, dtype=jnp.int32)
    block_of = causal_ids // half_rows
    source_row = (
        lookup(owner, block_of) * token_rows
        + lookup(late_side, block_of) * half_rows
        + causal_ids % half_rows
    )
    sorted_kv = jnp.take(all_kv, source_row, axis=0)
    early_block = lookup(pairs, ctx_id)
    late_block = 2 * n_ctx - 1 - early_block

    def query_positions(block_now):
        return block_now * half_rows + jnp.arange(half_rows, dtype=jnp.int32)

    def tile_total(block_now):
        return ((block_now + 1) * half_rows + key_tile - 1) // key_tile

    def key_slice(tile_no):
        tile_start = tile_no * key_tile
        key_value_tile = lax.dynamic_slice_in_dim(sorted_kv, tile_start, key_tile, 0)
        key_block_tile = key_value_tile[:, :KEY_FEATURES].reshape(
            key_tile, KEY_VALUE_HEADS, HEAD_SIZE
        )
        value_tile = key_value_tile[:, KEY_FEATURES:].reshape(key_tile, KEY_VALUE_HEADS, HEAD_SIZE)
        k_pos = tile_start + jnp.arange(key_tile, dtype=jnp.int32)
        return (tile_start, key_block_tile, value_tile, k_pos)

    def attend(query_half, block_now):
        q_pos = query_positions(block_now)
        query_group = query_half.reshape(half_rows, KEY_VALUE_HEADS, query_group_width, HEAD_SIZE)

        def tile_scores(tile_no):
            tile_start, key_block_tile, value_tile, k_pos = key_slice(tile_no)
            scores = score_scale * jnp.einsum(
                "qkgd,tkd->kgqt", query_group, key_block_tile, preferred_element_type=jnp.float32
            )
            visible = k_pos[None, :] <= q_pos[:, None]
            return (jnp.where(visible, scores, -jnp.inf), value_tile)

        def total_step(tile_no, state_carry):
            run_peak, run_total = state_carry
            scores, value_tile = tile_scores(tile_no)
            new_peak = jnp.maximum(run_peak, jnp.max(scores, -1))
            factor = jnp.exp(run_peak - new_peak)
            run_total = run_total * factor + jnp.sum(jnp.exp(scores - new_peak[..., None]), -1)
            return (new_peak, run_total)

        tile_count = tile_total(block_now)
        initial_state = (
            jnp.full((KEY_VALUE_HEADS, query_group_width, half_rows), -jnp.inf, jnp.float32),
            jnp.zeros((KEY_VALUE_HEADS, query_group_width, half_rows), jnp.float32),
        )
        run_peak, run_total = lax.fori_loop(0, tile_count, total_step, initial_state)
        log_total = run_peak + jnp.log(run_total)

        def value_step(tile_no, run_accum):
            scores, value_tile = tile_scores(tile_no)
            prob_bf = jnp.exp(scores - log_total[..., None]).astype(jnp.bfloat16)
            return run_accum + jnp.einsum(
                "kgqt,tkd->kgqd", prob_bf, value_tile, preferred_element_type=jnp.float32
            )

        run_accum = lax.fori_loop(
            0,
            tile_count,
            value_step,
            jnp.zeros((KEY_VALUE_HEADS, query_group_width, half_rows, HEAD_SIZE), jnp.float32),
        )
        context_half = jnp.transpose(run_accum, (2, 0, 1, 3)).reshape(half_rows, QW)
        return (context_half, log_total)

    query_flat = query_narrow.reshape(token_rows, QW)
    ctx_early, lse_early = attend(query_flat[:half_rows], early_block)
    ctx_late, lse_late = attend(query_flat[half_rows:], late_block)
    context_rows = jnp.concatenate([ctx_early, ctx_late], 0)
    context_bf = context_rows.astype(jnp.bfloat16)

    def by_feature_shard(rows):
        return jnp.transpose(rows.reshape(token_rows, n_wt, D // n_wt), (1, 0, 2))

    mid_rows = x_rows + jnp.dot(context_bf, wo_b, preferred_element_type=jnp.float32)
    gain_two_full = gain_two.astype(jnp.float32)
    inv_rms_two = lax.rsqrt(jnp.mean(mid_rows * mid_rows, -1, keepdims=True) + norm_eps)
    normed_two = (mid_rows * inv_rms_two * gain_two_full).astype(jnp.bfloat16)
    cot_bf = cot_rows.astype(jnp.bfloat16)
    normed_group, cot_group = (
        lax.all_gather(normed_two, "wt", axis=0, tiled=True),
        lax.all_gather(cot_bf, "wt", axis=0, tiled=True),
    )
    gate_pre = inner_dot(normed_group, wg_own)
    up_pre = inner_dot(normed_group, wu_own)
    hidden_bf = hidden_units(gate_pre, up_pre)
    out_terms = jnp.dot(hidden_bf, wd_own, preferred_element_type=jnp.float32)
    d_hidden = inner_dot(cot_group, wd_own)
    d_gate, d_up = gate_terms(gate_pre, up_pre, d_hidden)
    ff_grads = jnp.concatenate(
        [
            outer_dot(d_gate, normed_group).astype(jnp.bfloat16),
            outer_dot(d_up, normed_group).astype(jnp.bfloat16),
            outer_dot(hidden_bf, cot_group).astype(jnp.bfloat16),
        ],
        0,
    )
    piece_len = moment1.shape[1]
    ff_rows = ff_grads.shape[0]
    taken = min(ff_rows, (piece_len // D + 2 + 16 + 31) // 32 * 32)
    first_rows = ff_first_row(n_ctx, piece_len, prefix, ff_rows, taken)
    back_terms = jnp.dot(d_gate, wg_own, preferred_element_type=jnp.float32) + jnp.dot(
        d_up, wu_own, preferred_element_type=jnp.float32
    )
    ff_sum, d_norm_two, ff_terms = exchange(
        out_terms.reshape(n_wt, token_rows, D),
        back_terms.reshape(n_wt, token_rows, D),
        jnp.stack([ff_grads[row : row + taken] for row in first_rows]),
    )
    block_out = mid_rows + ff_sum
    grad_gain_two = jnp.sum(d_norm_two * mid_rows * inv_rms_two, 0)
    d_scaled_two = d_norm_two * gain_two_full
    d_mid = (
        cot_rows
        + inv_rms_two * d_scaled_two
        - mid_rows
        * (inv_rms_two * inv_rms_two * inv_rms_two)
        * jnp.mean(d_scaled_two * mid_rows, -1, keepdims=True)
    )
    d_mid_bf = d_mid.astype(jnp.bfloat16)
    context_gradient = inner_dot(d_mid_bf, wo_b)
    context_gradient_narrow = context_gradient.astype(jnp.bfloat16)
    delta_rows = jnp.sum(
        (context_gradient * context_rows).reshape(
            token_rows, KEY_VALUE_HEADS, query_group_width, HEAD_SIZE
        ),
        -1,
    )

    def attend_back(query_half, half_gradient, lse_half, delta_half, block_now, key_gradients):
        q_pos = query_positions(block_now)
        query_group = query_half.reshape(half_rows, KEY_VALUE_HEADS, query_group_width, HEAD_SIZE)
        group_gradient = half_gradient.reshape(
            half_rows, KEY_VALUE_HEADS, query_group_width, HEAD_SIZE
        )
        delta_t = jnp.transpose(delta_half, (1, 2, 0))[..., None]

        def tile_step(tile_no, state_carry):
            d_query, key_gradients = state_carry
            tile_start, key_block_tile, value_tile, k_pos = key_slice(tile_no)
            scores = score_scale * jnp.einsum(
                "qkgd,tkd->kgqt", query_group, key_block_tile, preferred_element_type=jnp.float32
            )
            visible = k_pos[None, :] <= q_pos[:, None]
            scores = jnp.where(visible, scores, -jnp.inf)
            prob_tile = jnp.where(visible, jnp.exp(scores - lse_half[..., None]), 0.0)
            prob_bf = prob_tile.astype(jnp.bfloat16)
            d_probs = jnp.einsum(
                "qkgd,tkd->kgqt", group_gradient, value_tile, preferred_element_type=jnp.float32
            )
            d_scores = (prob_tile * (d_probs - delta_t)).astype(jnp.bfloat16)
            d_query = d_query + score_scale * jnp.einsum(
                "kgqt,tkd->qkgd", d_scores, key_block_tile, preferred_element_type=jnp.float32
            )
            key_part = score_scale * jnp.einsum(
                "kgqt,qkgd->tkd", d_scores, query_group, preferred_element_type=jnp.float32
            )
            value_part = jnp.einsum(
                "kgqt,qkgd->tkd", prob_bf, group_gradient, preferred_element_type=jnp.float32
            )
            update = jnp.concatenate(
                [
                    key_part.reshape(key_tile, KEY_FEATURES),
                    value_part.reshape(key_tile, KEY_FEATURES),
                ],
                1,
            )
            current = lax.dynamic_slice_in_dim(key_gradients, tile_start, key_tile, 0)
            key_gradients = lax.dynamic_update_slice_in_dim(
                key_gradients, current + update, tile_start, 0
            )
            return (d_query, key_gradients)

        initial_state = (
            jnp.zeros((half_rows, KEY_VALUE_HEADS, query_group_width, HEAD_SIZE), jnp.float32),
            key_gradients,
        )
        return lax.fori_loop(0, tile_total(block_now), tile_step, initial_state)

    key_gradients = jnp.zeros((seq_len, 2 * KEY_FEATURES), jnp.float32)
    dq_early, key_gradients = attend_back(
        query_flat[:half_rows],
        context_gradient_narrow[:half_rows],
        lse_early,
        delta_rows[:half_rows],
        early_block,
        key_gradients,
    )
    dq_late, key_gradients = attend_back(
        query_flat[half_rows:],
        context_gradient_narrow[half_rows:],
        lse_late,
        delta_rows[half_rows:],
        late_block,
        key_gradients,
    )
    d_query_rot = jnp.concatenate([dq_early, dq_late], 0).reshape(
        token_rows, QUERY_HEADS, HEAD_SIZE
    )
    d_query = rotary_inverse(d_query_rot, cosine_table, sine_lookup).reshape(token_rows, QW)
    row_ids = jnp.arange(seq_len, dtype=jnp.int32)
    local_ids = row_ids % token_rows
    chosen = lookup(pairs, row_ids // token_rows)
    back_block = jnp.where(local_ids < half_rows, chosen, 2 * n_ctx - 1 - chosen)
    back_index = back_block * half_rows + local_ids % half_rows
    per_device = jnp.take(key_gradients, back_index, axis=0)
    owned_gradients = lax.psum_scatter(per_device, "ctx", scatter_dimension=0, tiled=True)
    key_gradient = rotary_inverse(
        owned_gradients[:, :KEY_FEATURES].reshape(token_rows, KEY_VALUE_HEADS, HEAD_SIZE),
        cosine_table,
        sine_lookup,
    ).reshape(token_rows, KEY_FEATURES)
    value_gradient = owned_gradients[:, KEY_FEATURES:]
    dq_bf = d_query.astype(jnp.bfloat16)
    dk_bf = key_gradient.astype(jnp.bfloat16)
    dv_bf = value_gradient.astype(jnp.bfloat16)
    d_norm = inner_dot(dq_bf, wq_b) + inner_dot(dk_bf, wk_b) + inner_dot(dv_bf, wv_b)
    grad_gain = jnp.sum(d_norm * x_rows * inv_rms, 0)
    d_scaled = d_norm * gain_full
    d_input = inv_rms * d_scaled - x_rows * (inv_rms * inv_rms * inv_rms) * jnp.mean(
        d_scaled * x_rows, -1, keepdims=True
    )
    input_grad = d_mid + d_input
    feature_cols, context_cols, mid_group, query_grads, key_value_grads = gather_wt(
        [
            by_feature_shard(normed),
            by_feature_shard(context_bf),
            d_mid_bf,
            dq_bf,
            jnp.concatenate([dk_bf, dv_bf], 1),
        ],
        n_wt,
        2,
        4,
    )
    attn_grads = jnp.concatenate(
        [
            outer_dot(feature_cols, query_grads),
            outer_dot(feature_cols, key_value_grads),
            outer_dot(context_cols, mid_group),
        ],
        1,
    ).astype(jnp.bfloat16)
    attn_part = attn_grads.shape[0] // n_ctx
    vectors = jnp.concatenate(
        [
            grad_gain,
            jnp.sum(dq_bf.astype(jnp.float32), 0),
            jnp.sum(dk_bf.astype(jnp.float32), 0),
            jnp.sum(dv_bf.astype(jnp.float32), 0),
            grad_gain_two,
        ]
    )
    vectors = jnp.pad(vectors, (0, -vectors.shape[0] % 1024)).reshape(-1, LANES)
    attn_sum, vector_sums = reduce_attention(
        attn_grads.reshape(n_ctx, attn_part, MATRIX_COLS),
        vectors,
        n_wt,
        -(-prefix // piece_len),
    )
    attn_sum = attn_sum.reshape(n_ctx * attn_part, MATRIX_COLS)
    vector_sums = vector_sums.reshape(-1)
    small = []
    left = 0
    for full in (D, QW, KEY_FEATURES, KEY_FEATURES, D):
        small.append(
            lax.dynamic_slice_in_dim(vector_sums, left + wt_id * (full // n_wt), full // n_wt, 0)
        )
        left += full
    small, row_of_small = small_rows(small, [bounds[number] for number in vector_numbers])
    piece_start = ctx_id * piece_len
    flat_start = piece_start - D * lookup(jnp.array(first_rows, jnp.int32), ctx_id)
    own_row = piece_start // LANES // 8 * 8
    out_rows = (piece_len + LANES * 64 - 1) // (LANES * 64) * 64
    own_rows = lax.dynamic_slice_in_dim(flat_params, own_row, out_rows + 16, 0)
    place = jnp.stack(
        [
            flat_start // LANES,
            flat_start % LANES,
            piece_start // LANES - own_row,
            piece_start % LANES,
            piece_start,
        ]
    ).astype(jnp.int32)
    tail = ((0, 0), (0, out_rows * LANES - piece_len))
    updated = assemble(
        n_wt,
        small,
        row_of_small,
        attn_sum,
        ff_terms,
        own_rows,
        jnp.pad(moment1, tail).reshape(out_rows, LANES),
        jnp.pad(moment2, tail).reshape(out_rows, LANES),
        place,
    )
    param_grad, new_params, new_moment1, new_moment2 = [
        rows.reshape(1, -1)[:, :piece_len] for rows in updated
    ]
    return (
        block_out.reshape(1, token_rows, D),
        input_grad.reshape(1, token_rows, D),
        param_grad,
        new_params,
        new_moment1,
        new_moment2,
    )


def solution(mesh):
    in_specs = (
        P("wt", "ctx", None),
        P("wt", "ctx", None),
        P(),
        P("wt", "ctx"),
        P("wt", None),
        P("wt", "ctx"),
        P("wt", "ctx"),
    )
    out_specs = (
        P("wt", "ctx", None),
        P("wt", "ctx", None),
        P("wt", "ctx"),
        P("wt", "ctx"),
        P("wt", "ctx"),
        P("wt", "ctx"),
    )
    return jax.shard_map(body, mesh=mesh, in_specs=in_specs, out_specs=out_specs, check_vma=False)
```
